256 devices in a mesh: section: 4 (over x), dom: 64 (over y, z, core).
Axes of the slice: x: 4, y: 4, z: 8, core: 2. Of those that a mesh axis runs over, the one named last changes fastest.
Arguments:
- layer_inputs: bfloat16 [4, 1, 24576, 512], P('section', None, 'dom'), may hold values from -6 to 6
- top_grad: bfloat16 [1, 24576, 512], P(None, 'dom'), may hold values from -6 to 6
- w_qkv: bfloat16 [4, 512, 1536], P('section')
- w_out: bfloat16 [4, 512, 512], P('section'), may hold values from -0.25 to 0.25
- neighbours: int32 [192, 3], P('dom'), may hold values from -1 to 191, as said below
Outputs:
- input_grads: bfloat16 [4, 1, 24576, 512], P('section', None, 'dom')
- qkv_grad: float32 [4, 512, 1536], P('section', 'dom')
- out_grad: float32 [4, 512, 512], P('section', 'dom')
The draws below stay inside these ranges and needn't reach their ends.
Inputs may be any that keep to these rules, and one draw needn't show every extreme that they name: `neighbours`: entry 0 of block b is b; the other entries name distinct blocks (b + o) mod 192 with 0 < |o| <= 1, then -1 to the end of the row. The first block of every index of dom lists 3 blocks.
All inputs are finite; a program needn't handle non-finite values.
Results may differ from the reference program's by a relative error of at most 0.017.
Values may be sent and summed in bfloat16 or wider, within the bound.
A program may use at most 128 MiB of HBM per device.

```python
import jax
import jax.numpy as jnp
from jax import lax

D = 512
HEADS = 8
TILE = 128
KMAX = 3
HALO = 1
BLK_DEV = 3
MICRO = 1
LAYERS = 4
BLOCKS = 192
NODES = 24576
N_DOM = 64


def draw_w_qkv(key, part):
    first = jax.random.fold_in(key, 0)
    base = jax.random.normal(first, (LAYERS, D, 3 * D), jnp.float32) * D ** (-0.5)
    return base.astype(jnp.bfloat16)


def draw_neighbours(key, part):
    first, second, third = jax.random.split(key, 3)
    devices = BLOCKS // BLK_DEV
    level = jax.random.randint(first, (devices,), 1, KMAX + 1)
    level = jnp.repeat(level, BLK_DEV)
    jitter = jax.random.randint(second, (BLOCKS,), -1, 2)
    count = jnp.clip(level + jitter, 1, KMAX)
    place = jnp.arange(BLOCKS)
    count = jnp.where(place % BLK_DEV == 0, KMAX, count)
    count = count.at[1].set(1)
    offsets = jnp.concatenate([jnp.arange(-HALO, 0), jnp.arange(1, HALO + 1)])
    scores = jax.random.randint(third, (BLOCKS, 2 * HALO), 0, 1 << 20) * (2 * HALO) + jnp.arange(2 * HALO)[None, :]
    order = jnp.argsort(scores, axis=1)
    chosen = offsets[order[:, :KMAX - 1]]
    ids = (place[:, None] + chosen) % BLOCKS
    keep = jnp.arange(1, KMAX)[None, :] < count[:, None]
    rest = jnp.where(keep, ids, -1)
    return jnp.concatenate([place[:, None], rest], axis=1).astype(jnp.int32)


def block_scale(rng, shape, cuts, low, top_value):
    factor_of, own = 1.0, jax.random.fold_in(rng, 6)
    for position, blocks in cuts:
        heights = jnp.exp(jax.random.uniform(jax.random.fold_in(own, position), (blocks,), jnp.float32, low / len(cuts), top_value / len(cuts)))
        factor_of = factor_of * jnp.repeat(heights, shape[position] // blocks).reshape([-1 if axis == position else 1 for axis in range(len(shape))])
    return factor_of


def gaussian(rng, shape, deviation, limit, cuts=(), dtype=jnp.bfloat16):
    result = jax.random.normal(rng, shape, jnp.float32) * deviation
    if len(cuts) > 0:
        result = block_scale(rng, shape, cuts, -0.22, 0.18) * result
    return jnp.clip(result, min=-limit, max=limit).astype(dtype)


def setup_inputs(seed: int = 0) -> dict:
    arg_keys = jax.random.split(jax.random.key(seed), 6)
    return {
        "layer_inputs": gaussian(arg_keys[0], (LAYERS, MICRO, NODES, D), 1.0, 6.0, ((0, 4), (2, 64))),
        "top_grad": gaussian(arg_keys[1], (MICRO, NODES, D), 1.0, 6.0, ((1, 64),)),
        "w_qkv": draw_w_qkv(jax.random.fold_in(arg_keys[5], 71), 0),
        "w_out": gaussian(arg_keys[3], (LAYERS, D, D), D ** -0.5, 0.25, ((0, 4),)),
        "neighbours": draw_neighbours(jax.random.fold_in(arg_keys[5], 71), 0),
    }


def layer_reference(x, g, w_qkv, w_out, neighbours):
    blocks = x.shape[0] // TILE
    width = x.shape[1]
    hdim = width // HEADS
    scale = 1.0 / hdim ** 0.5
    xf = x.astype(jnp.float32)
    mean_value = lax.optimization_barrier(jnp.mean(xf, axis=-1, keepdims=True))
    centered_input = xf - mean_value
    inverse_deviation = jax.lax.rsqrt(lax.optimization_barrier(jnp.mean(centered_input * centered_input, axis=-1, keepdims=True)) + 1e-05)
    normalized_input = centered_input * inverse_deviation
    normed_rows = normalized_input.astype(jnp.bfloat16)
    qkv = jnp.dot(normed_rows, w_qkv, preferred_element_type=jnp.float32).astype(jnp.bfloat16)
    qkv = qkv.reshape(blocks, TILE, 3 * width)
    query = qkv[..., :width].reshape(blocks, TILE, HEADS, hdim)
    keyval = qkv[..., width:]
    valid = neighbours >= 0
    where_at = jnp.where(valid, neighbours, 0).astype(jnp.int32)
    tiles = keyval[where_at]
    keys = tiles[..., :width].reshape(blocks, KMAX * TILE, HEADS, hdim)
    values = tiles[..., width:].reshape(blocks, KMAX * TILE, HEADS, hdim)
    mask = jnp.repeat(valid, TILE, axis=1)[:, None, None, :]
    scores = jnp.einsum('bqhd,bkhd->bhqk', query.astype(jnp.float32), keys.astype(jnp.float32)) * scale
    scores = jnp.where(mask, scores, -1e+30)
    top = lax.optimization_barrier(jnp.max(scores, axis=-1, keepdims=True))
    expo = jnp.exp(scores - top)
    probs = expo / lax.optimization_barrier(jnp.sum(expo, axis=-1, keepdims=True))
    probs_b = probs.astype(jnp.bfloat16)
    attn = jnp.einsum('bhqk,bkhd->bqhd', probs_b.astype(jnp.float32), values.astype(jnp.float32)).astype(jnp.bfloat16)
    attn = attn.reshape(blocks * TILE, width)
    out_term = jnp.dot(attn.T, g, preferred_element_type=jnp.float32)
    d_attn = jnp.dot(g, w_out.T, preferred_element_type=jnp.float32).astype(jnp.bfloat16)
    d_attn = d_attn.reshape(blocks, TILE, HEADS, hdim)
    d_prob = jnp.einsum('bqhd,bkhd->bhqk', d_attn.astype(jnp.float32), values.astype(jnp.float32))
    d_score = (probs * (d_prob - lax.optimization_barrier(jnp.sum(d_prob * probs, axis=-1, keepdims=True))) * scale).astype(jnp.bfloat16)
    d_query = jnp.einsum('bhqk,bkhd->bqhd', d_score.astype(jnp.float32), keys.astype(jnp.float32))
    d_keys = jnp.einsum('bhqk,bqhd->bkhd', d_score.astype(jnp.float32), query.astype(jnp.float32))
    d_values = jnp.einsum('bhqk,bqhd->bkhd', probs_b.astype(jnp.float32), d_attn.astype(jnp.float32))
    d_tiles = jnp.concatenate([d_keys.reshape(blocks, KMAX, TILE, width), d_values.reshape(blocks, KMAX, TILE, width)], axis=-1)
    source = (jnp.arange(blocks) // BLK_DEV).astype(jnp.int32)[:, None]
    target = (where_at // BLK_DEV).astype(jnp.int32)
    same = valid & (source == target)
    from_next = valid & (source == (target + 1) % N_DOM)
    from_prev = valid & (source == (target - 1) % N_DOM)

    def collect(select):
        terms = (d_tiles * select[:, :, None, None].astype(jnp.float32)).reshape(blocks * KMAX, TILE, 2 * width)
        return jax.ops.segment_sum(terms, where_at.reshape(-1), num_segments=blocks)
    d_keyval = collect(same) + collect(from_next).astype(jnp.bfloat16).astype(jnp.float32)
    d_keyval = d_keyval + collect(from_prev).astype(jnp.bfloat16).astype(jnp.float32)
    d_qkv = jnp.concatenate([d_query.reshape(blocks, TILE, width), d_keyval], axis=-1).astype(jnp.bfloat16)
    d_qkv = d_qkv.reshape(blocks * TILE, 3 * width)
    qkv_term = jnp.dot(normed_rows.T, d_qkv, preferred_element_type=jnp.float32)
    normed_gradient = jnp.dot(d_qkv, w_qkv.T, preferred_element_type=jnp.float32)
    layernorm_gradient = inverse_deviation * (normed_gradient - lax.optimization_barrier(jnp.mean(normed_gradient, axis=-1, keepdims=True)) - normalized_input * lax.optimization_barrier(jnp.mean(normed_gradient * normalized_input, axis=-1, keepdims=True)))
    d_input = (g.astype(jnp.float32) + layernorm_gradient).astype(jnp.bfloat16)
    return (d_input, qkv_term, out_term)

def reference(layer_inputs, top_grad, w_qkv, w_out, neighbours):
    grads = [[None] * MICRO for layer in range(LAYERS)]
    qkv_sums = [jnp.zeros(w_qkv.shape[1:], jnp.float32) for layer in range(LAYERS)]
    out_sums = [jnp.zeros(w_out.shape[1:], jnp.float32) for layer in range(LAYERS)]
    for micro_idx in range(MICRO):
        g = top_grad[micro_idx]
        for layer in range(LAYERS - 1, -1, -1):
            g, qkv_term, out_term = layer_reference(layer_inputs[layer, micro_idx], g, w_qkv[layer], w_out[layer], neighbours)
            grads[layer][micro_idx] = g
            qkv_sums[layer] = qkv_sums[layer] + qkv_term
            out_sums[layer] = out_sums[layer] + out_term
    input_grads = jnp.stack([jnp.stack(row) for row in grads])
    return (input_grads, jnp.stack(qkv_sums), jnp.stack(out_sums))
```

```python
import jax
import jax.numpy as jnp
from jax import lax
from jax.experimental import pallas as pl
from jax.experimental.pallas import tpu as pltpu
from jax.sharding import PartitionSpec as P

SEC = 4
NY, NZ, NC = 4, 8, 2
DOM = NY * NZ * NC
D = 512
HEADS = 8
HDIM = D // HEADS
PAIRS = HEADS // 2
TILE = 128
BLK = 3
KEYS = 3 * TILE
ROWS = BLK * TILE
EXT = ROWS + 2 * TILE
COLS = 4
SCALE = 1.0 / HDIM**0.5
BF = jnp.bfloat16
F32 = jnp.float32
MESH = pl.DeviceIdType.MESH


def dot(a, b, ca, cb):
    return lax.dot_general(a, b, (((ca,), (cb,)), ((), ())), preferred_element_type=F32)


def body(
    nbr, x_hbm, g_hbm, wq_hbm, wo_hbm, gout_hbm, dwq_ref, dwo_ref,
    x_v, wq, wo, g_v, xhat, inv_v, xn, xnT, q2, kv, kT, pr, attnT, da2, acc,
    rim_lo, rim_hi, rim_next, rim_prev, dqkv, gout,
    gs, cs, cr, ys, yr, zs, zr,
    in_sem, out_sem, halo_s, halo_r, rim_s, rim_r, g_s, g_r,
    cs_s, cs_r, y_s, y_r, z_s, z_r,
):
    sec = lax.axis_index("section")
    dom = lax.axis_index("dom")
    y = lax.div(dom, NZ * NC)
    z = lax.rem(lax.div(dom, NC), NZ)
    c = lax.rem(dom, NC)
    nxt = lax.rem(dom + 1, DOM)
    prv = lax.rem(dom + DOM - 1, DOM)
    partner = dom + 1 - 2 * c
    before = lax.rem(sec + SEC - 1, SEC)
    after = lax.rem(sec + 1, SEC)

    def y_dev(o):
        return lax.rem(y + o, NY) * (NZ * NC) + z * NC + c

    def z_dev(o):
        return y * (NZ * NC) + lax.rem(z + o, NZ) * NC + c

    load_x = pltpu.make_async_copy(x_hbm, x_v, in_sem.at[0])
    load_wq = pltpu.make_async_copy(wq_hbm, wq, in_sem.at[1])
    load_wo = pltpu.make_async_copy(wo_hbm, wo, in_sem.at[2])
    load_g = pltpu.make_async_copy(g_hbm, g_v, in_sem.at[3])
    load_x.start()
    load_wq.start()
    load_wo.start()

    @pl.when(sec == SEC - 1)
    def _():
        load_g.start()

    barrier = pltpu.get_barrier_semaphore()
    peers = [(sec, nxt), (sec, prv), (sec, partner), (before, dom), (after, dom)]
    peers += [(sec, y_dev(o)) for o in range(1, NY)]
    peers += [(sec, z_dev(o)) for o in range(1, NZ)]
    for peer in peers:
        pl.semaphore_signal(barrier, inc=1, device_id=peer, device_id_type=MESH)

    lane = lax.broadcasted_iota(jnp.int32, (1, TILE), 1)
    m0 = jnp.where(lane < HDIM, 1.0, 0.0)
    m1 = 1.0 - m0

    load_x.wait()
    for b in range(BLK):
        rows = pl.ds(b * TILE, TILE)
        xf = x_v[rows, :].astype(F32)
        cen = xf - jnp.mean(xf, axis=-1, keepdims=True)
        inv = lax.rsqrt(jnp.mean(cen * cen, axis=-1, keepdims=True) + 1e-05)
        xh = cen * inv
        xhat[rows, :] = xh
        inv_v[rows, :] = jnp.broadcast_to(inv, (TILE, TILE))
        xn[rows, :] = xh.astype(BF)

    load_wq.wait()
    for h in range(2):
        part = dot(xn[...], wq[:, (1 + h) * D : (2 + h) * D], 1, 0)
        kv[TILE : TILE + ROWS, h * D : (h + 1) * D] = part.astype(BF)
    pl.semaphore_wait(barrier, len(peers))
    halo_up = pltpu.make_async_remote_copy(
        kv.at[pl.ds(ROWS, TILE)], kv.at[pl.ds(0, TILE)], halo_s.at[0], halo_r.at[0],
        device_id=(sec, nxt), device_id_type=MESH,
    )
    halo_dn = pltpu.make_async_remote_copy(
        kv.at[pl.ds(TILE, TILE)], kv.at[pl.ds(TILE + ROWS, TILE)], halo_s.at[1], halo_r.at[1],
        device_id=(sec, prv), device_id_type=MESH,
    )
    halo_up.start()
    halo_dn.start()

    qs = dot(xn[...], wq[:, 0:D], 1, 0).astype(BF).astype(F32) * SCALE
    for b in range(BLK):
        for p in range(PAIRS):
            qb = qs[b * TILE : (b + 1) * TILE, p * TILE : (p + 1) * TILE]
            q2[b * PAIRS + p, 0:TILE, :] = (qb * m0).astype(BF)
            q2[b * PAIRS + p, TILE:, :] = (qb * m1).astype(BF)

    def forward(b):
        here = dom * BLK + b
        low = lax.rem(here + DOM * BLK - 1, DOM * BLK)
        high = lax.rem(here + 1, DOM * BLK)
        n1 = jnp.full((TILE, 2 * TILE), nbr[b, 1], jnp.int32)
        n2 = jnp.full((TILE, 2 * TILE), nbr[b, 2], jnp.int32)
        has_low = (n1 == low) | (n2 == low)
        has_high = (n1 == high) | (n2 == high)
        for p in range(PAIRS):
            keys = kv[b * TILE : b * TILE + KEYS, p * TILE : (p + 1) * TILE]
            vals = kv[b * TILE : b * TILE + KEYS, D + p * TILE : D + (p + 1) * TILE]
            s = dot(keys, q2[b * PAIRS + p], 1, 1)
            s = jnp.concatenate(
                [
                    jnp.where(has_low, s[0:TILE], -1e30),
                    s[TILE : 2 * TILE],
                    jnp.where(has_high, s[2 * TILE :], -1e30),
                ],
                axis=0,
            )
            top = jnp.max(s, axis=0, keepdims=True)
            e = jnp.exp(s - top)
            pb = (e * (1.0 / jnp.sum(e, axis=0, keepdims=True))).astype(BF)
            pr[b * PAIRS + p] = pb
            o = dot(vals, pb, 0, 0)
            attnT[p * TILE : p * TILE + HDIM, b * TILE : (b + 1) * TILE] = o[
                0:HDIM, 0:TILE
            ].astype(BF)
            attnT[p * TILE + HDIM : (p + 1) * TILE, b * TILE : (b + 1) * TILE] = o[
                HDIM:, TILE:
            ].astype(BF)

    forward(1)
    halo_up.wait_recv()
    forward(0)
    halo_dn.wait_recv()
    forward(2)
    for e in range(EXT // TILE):
        kT[:, e * TILE : (e + 1) * TILE] = kv[e * TILE : (e + 1) * TILE, 0:D].T
    xnT[...] = xn[...].T
    load_wo.wait()

    def g_copy(b):
        return pltpu.make_async_remote_copy(
            gout.at[b], g_v.at[b], g_s.at[b], g_r.at[b],
            device_id=(before, dom), device_id_type=MESH,
        )

    rim_dn = pltpu.make_async_remote_copy(
        rim_lo, rim_next, rim_s.at[0], rim_r.at[0], device_id=(sec, prv), device_id_type=MESH
    )
    rim_up = pltpu.make_async_remote_copy(
        rim_hi, rim_prev, rim_s.at[1], rim_r.at[1], device_id=(sec, nxt), device_id_type=MESH
    )

    @pl.when(sec == SEC - 1)
    def _():
        load_g.wait()

    started = []

    def put(b, t, cols, val):
        rows = slice(t * TILE, (t + 1) * TILE)
        if t in started[-1][1]:
            acc[rows, cols] = acc[rows, cols] + val
        else:
            acc[rows, cols] = val

    done = set()
    for b in (0, 2, 1):
        @pl.when(sec < SEC - 1)
        def _():
            g_copy(b).wait_recv()

        da = dot(g_v[b], wo[...], 1, 1).astype(BF).astype(F32)
        for p in range(PAIRS):
            db = da[:, p * TILE : (p + 1) * TILE]
            da2[b * PAIRS + p, 0:TILE, :] = (db * m0).astype(BF)
            da2[b * PAIRS + p, TILE:, :] = (db * m1).astype(BF)
        started.append((b, set(done)))
        for p in range(PAIRS):
            vals = kv[b * TILE : b * TILE + KEYS, D + p * TILE : D + (p + 1) * TILE]
            d2 = da2[b * PAIRS + p]
            pb = pr[b * PAIRS + p]
            dp = dot(vals, d2, 1, 1)
            pf = pb.astype(F32)
            delta = jnp.sum(dp * pf, axis=0, keepdims=True)
            ds = (pf * (dp - delta)).astype(BF)
            dv = dot(pb, d2, 1, 0)
            dk = dot(ds, q2[b * PAIRS + p], 1, 0)
            for t in range(3):
                rows = slice(t * TILE, (t + 1) * TILE)
                put(b, b + t, slice(p * TILE, (p + 1) * TILE), dk[rows])
                put(b, b + t, slice(D + p * TILE, D + (p + 1) * TILE), dv[rows])
            dq = dot(kT[p * TILE : (p + 1) * TILE, b * TILE : b * TILE + KEYS], ds, 1, 0)
            dq = jnp.concatenate([dq[0:HDIM, 0:TILE], dq[HDIM:, TILE:]], axis=0)
            dqkv[b * TILE : (b + 1) * TILE, p * TILE : (p + 1) * TILE] = (dq.T * SCALE).astype(BF)
        done |= {b, b + 1, b + 2}
        if b == 0:
            rim_lo[...] = acc[0:TILE, :].astype(BF)
            rim_dn.start()
        if b == 2:
            rim_hi[...] = acc[EXT - TILE :, :].astype(BF)
            rim_up.start()

    for b in (0, 2, 1):
        rows = pl.ds(b * TILE, TILE)
        dkv = acc[(b + 1) * TILE : (b + 2) * TILE, :]
        if b == 0:
            rim_up.wait_recv()
            dkv = dkv + rim_prev[...].astype(F32)
        if b == 2:
            rim_dn.wait_recv()
            dkv = dkv + rim_next[...].astype(F32)
        dqkv[rows, D:] = dkv.astype(BF)
        dn = dot(dqkv[rows, :], wq[...], 1, 1)
        xh = xhat[rows, :]
        inv = inv_v[rows, 0:1]
        ln = inv * (
            dn
            - jnp.mean(dn, axis=-1, keepdims=True)
            - xh * jnp.mean(dn * xh, axis=-1, keepdims=True)
        )
        gout[b] = (g_v[b].astype(F32) + ln).astype(BF)

        @pl.when(sec > 0)
        def _():
            g_copy(b).start()

    store_g = pltpu.make_async_copy(gout, gout_hbm, out_sem)
    store_g.start()

    def c_copy(j):
        return pltpu.make_async_remote_copy(
            cs.at[j], cr.at[j], cs_s.at[j], cs_r.at[j],
            device_id=(sec, partner), device_id_type=MESH,
        )

    def y_copy(j, o):
        return pltpu.make_async_remote_copy(
            ys.at[j, o - 1], yr.at[j, o - 1], y_s.at[j, o - 1], y_r.at[j, o - 1],
            device_id=(sec, y_dev(o)), device_id_type=MESH,
        )

    def z_copy(j, o):
        return pltpu.make_async_remote_copy(
            zs.at[j, o - 1], zr.at[j, o - 1], z_s.at[j, o - 1], z_r.at[j, o - 1],
            device_id=(sec, z_dev(o)), device_id_type=MESH,
        )

    half = NY * NZ * 8
    order = (3, 0, 1, 2)
    for j in order:
        if j == 3:
            full = dot(attnT[...], g_v[...].reshape(ROWS, D), 1, 0)
        else:
            full = dot(xnT[...], dqkv[:, j * D : (j + 1) * D], 1, 0)
        gs[j] = full.reshape(NY * NZ, NC, 8, D)
        cs[j] = gs[j, :, 1 - c].reshape(half, D).astype(BF)
        c_copy(j).start()
    for j in order:
        c_copy(j).wait_recv()
        summed = gs[j, :, c] + cr[j].astype(F32).reshape(NY * NZ, 8, D)
        gs[j, :, 0] = summed
        for o in range(1, NY):
            to = lax.rem(y + o, NY)
            ys[j, o - 1] = gs[j, pl.ds(to * NZ, NZ), 0].reshape(NZ * 8, D).astype(BF)
            y_copy(j, o).start()
    for j in order:
        mine = gs[j, pl.ds(y * NZ, NZ), 0]
        for o in range(1, NY):
            y_copy(j, o).wait_recv()
            mine = mine + yr[j, o - 1].astype(F32).reshape(NZ, 8, D)
        gs[j, 0:NZ, 1] = mine
        for o in range(1, NZ):
            to = lax.rem(z + o, NZ)
            piece = gs[j, to, 1]
            zs[j, o - 1] = jnp.concatenate(
                [piece[:, 0 : D // 2], piece[:, D // 2 :]], axis=0
            ).astype(BF)
            z_copy(j, o).start()
    for j in order:
        own = gs[j, z, 1]
        total = jnp.concatenate([own[:, 0 : D // 2], own[:, D // 2 :]], axis=0)
        for o in range(1, NZ):
            z_copy(j, o).wait_recv()
            total = total + zr[j, o - 1].astype(F32)
        total = jnp.concatenate([total[0:8], total[8:16]], axis=1)
        if j == 3:
            dwo_ref[...] = total
        else:
            dwq_ref[:, j * D : (j + 1) * D] = total

    halo_up.wait_send()
    halo_dn.wait_send()
    rim_up.wait_send()
    rim_dn.wait_send()

    @pl.when(sec > 0)
    def _():
        for b in range(BLK):
            g_copy(b).wait_send()

    for j in range(COLS):
        c_copy(j).wait_send()
        for o in range(1, NY):
            y_copy(j, o).wait_send()
        for o in range(1, NZ):
            z_copy(j, o).wait_send()
    store_g.wait()


def local(layer_inputs, top_grad, w_qkv, w_out, neighbours):
    vm = pltpu.VMEM
    sem = pltpu.SemaphoreType.DMA
    anyspec = pl.BlockSpec(memory_space=pl.ANY)
    vspec = pl.BlockSpec(memory_space=pltpu.VMEM)
    gin, dwq, dwo = pl.pallas_call(
        body,
        out_shape=(
            jax.ShapeDtypeStruct((BLK, TILE, D), BF),
            jax.ShapeDtypeStruct((D // DOM, 3 * D), F32),
            jax.ShapeDtypeStruct((D // DOM, D), F32),
        ),
        in_specs=[pl.BlockSpec(memory_space=pltpu.SMEM)] + [anyspec] * 4,
        out_specs=(anyspec, vspec, vspec),
        scratch_shapes=[
            vm((ROWS, D), BF),
            vm((D, 3 * D), BF),
            vm((D, D), BF),
            vm((BLK, TILE, D), BF),
            vm((ROWS, D), F32),
            vm((ROWS, TILE), F32),
            vm((ROWS, D), BF),
            vm((D, ROWS), BF),
            vm((BLK * PAIRS, 2 * TILE, TILE), BF),
            vm((EXT, 2 * D), BF),
            vm((D, EXT), BF),
            vm((BLK * PAIRS, KEYS, 2 * TILE), BF),
            vm((D, ROWS), BF),
            vm((BLK * PAIRS, 2 * TILE, TILE), BF),
            vm((EXT, 2 * D), F32),
            vm((TILE, 2 * D), BF),
            vm((TILE, 2 * D), BF),
            vm((TILE, 2 * D), BF),
            vm((TILE, 2 * D), BF),
            vm((ROWS, 3 * D), BF),
            vm((BLK, TILE, D), BF),
            vm((COLS, NY * NZ, NC, 8, D), F32),
            vm((COLS, NY * NZ * 8, D), BF),
            vm((COLS, NY * NZ * 8, D), BF),
            vm((COLS, NY - 1, NZ * 8, D), BF),
            vm((COLS, NY - 1, NZ * 8, D), BF),
            vm((COLS, NZ - 1, 16, D // 2), BF),
            vm((COLS, NZ - 1, 16, D // 2), BF),
            sem((4,)), sem(()),
            sem((2,)), sem((2,)), sem((2,)), sem((2,)), sem((BLK,)), sem((BLK,)),
            sem((COLS,)), sem((COLS,)),
            sem((COLS, NY - 1)), sem((COLS, NY - 1)),
            sem((COLS, NZ - 1)), sem((COLS, NZ - 1)),
        ],
        compiler_params=pltpu.CompilerParams(
            collective_id=0, has_side_effects=True, vmem_limit_bytes=60 << 20
        ),
        name="layer_backward",
    )(
        neighbours,
        layer_inputs.reshape(ROWS, D),
        top_grad.reshape(BLK, TILE, D),
        w_qkv.reshape(D, 3 * D),
        w_out.reshape(D, D),
    )
    return (gin.reshape(1, 1, ROWS, D), dwq[None], dwo[None])


def solution(mesh):
    placed = (
        P("section", None, "dom", None),
        P(None, "dom", None),
        P("section", None, None),
        P("section", None, None),
        P("dom", None),
    )
    return jax.shard_map(
        local,
        mesh=mesh,
        in_specs=placed,
        out_specs=(
            P("section", None, "dom", None),
            P("section", "dom", None),
            P("section", "dom", None),
        ),
        check_vma=False,
    )
```

```python
import jax
import jax.numpy as jnp
from jax import lax
from jax.experimental import pallas as pl
from jax.experimental.pallas import tpu as pltpu
from jax.sharding import PartitionSpec as P

SEC = 4
NY, NZ, NC = 4, 8, 2
DOM = NY * NZ * NC
D = 512
HEADS = 8
HDIM = D // HEADS
PAIRS = HEADS // 2
TILE = 128
BLK = 3
KEYS = 3 * TILE
ROWS = BLK * TILE
EXT = ROWS + 2 * TILE
HALF = NY * NZ * 8
SCALE = 1.0 / HDIM**0.5
BF = jnp.bfloat16
F32 = jnp.float32
MESH = pl.DeviceIdType.MESH
CHUNKS = ((1536, 512, "z"), (0, 512, "y"), (512, 512, "y"), (1024, 256, "y"), (1280, 256, "z"))


def dot(a, b, ca, cb):
    return lax.dot_general(a, b, (((ca,), (cb,)), ((), ())), preferred_element_type=F32)


def body(
    nbr, x_hbm, g_hbm, wq_hbm, wo_hbm, gout_hbm, dwq_ref, dwo_ref,
    x_v, wq, wo, g_v, xhat, inv_v, xn, xnT, q2, kv, kvT, pr, attnT, da2, acc,
    rim_lo, rim_hi, rim_l, rim_r, dqkv, gout,
    in_sem, out_sem, halo_s, halo_r, rim_ss, rim_rs, g_s, g_r, cores, firsts, seconds,
):
    sec = lax.axis_index("section")
    dom = lax.axis_index("dom")
    y = lax.div(dom, NZ * NC)
    z = lax.rem(lax.div(dom, NC), NZ)
    c = lax.rem(dom, NC)
    left = lax.rem(dom + DOM - 1 + 2 * c, DOM)
    partner = dom + 1 - 2 * c
    before = lax.rem(sec + SEC - 1, SEC)
    after = lax.rem(sec + 1, SEC)

    def place(i):
        return i + c * (2 - 2 * i)

    def y_dev(o):
        return lax.rem(y + o, NY) * (NZ * NC) + z * NC + c

    def z_dev(o):
        return y * (NZ * NC) + lax.rem(z + o, NZ) * NC + c

    load_x = [pltpu.make_async_copy(x_hbm.at[place(i)], x_v.at[i], in_sem.at[i]) for i in range(BLK)]
    load_g = [
        pltpu.make_async_copy(g_hbm.at[place(i)], g_v.at[i], in_sem.at[BLK + i]) for i in range(BLK)
    ]
    load_wq = pltpu.make_async_copy(wq_hbm, wq, in_sem.at[2 * BLK])
    load_wo = pltpu.make_async_copy(wo_hbm, wo, in_sem.at[2 * BLK + 1])
    for copy in load_x:
        copy.start()
    load_wq.start()
    load_wo.start()

    @pl.when(sec == SEC - 1)
    def _():
        for copy in load_g:
            copy.start()

    barrier = pltpu.get_barrier_semaphore()
    peers = [(sec, left), (sec, partner), (before, dom), (after, dom)]
    peers += [(sec, y_dev(o)) for o in range(1, NY)]
    peers += [(sec, z_dev(o)) for o in range(1, NZ)]
    for peer in peers:
        pl.semaphore_signal(barrier, inc=1, device_id=peer, device_id_type=MESH)

    lane = lax.broadcasted_iota(jnp.int32, (1, TILE), 1)
    m0 = jnp.where(lane < HDIM, 1.0, 0.0)
    m1 = 1.0 - m0

    for b in range(BLK):
        load_x[b].wait()
        rows = pl.ds(b * TILE, TILE)
        xf = x_v[b].astype(F32)
        cen = xf - jnp.mean(xf, axis=-1, keepdims=True)
        inv = lax.rsqrt(jnp.mean(cen * cen, axis=-1, keepdims=True) + 1e-05)
        xh = cen * inv
        xhat[rows, :] = xh
        inv_v[rows, :] = jnp.broadcast_to(inv, (TILE, TILE))
        xn[rows, :] = xh.astype(BF)

    load_wq.wait()
    for h in range(2):
        part = dot(xn[...], wq[:, (1 + h) * D : (2 + h) * D], 1, 0)
        kv[TILE : TILE + ROWS, h * D : (h + 1) * D] = part.astype(BF)
    pl.semaphore_wait(barrier, len(peers))
    halo_l = pltpu.make_async_remote_copy(
        kv.at[pl.ds(TILE, TILE)], kv.at[pl.ds(0, TILE)], halo_s.at[0], halo_r.at[0],
        device_id=(sec, left), device_id_type=MESH,
    )
    halo_h = pltpu.make_async_remote_copy(
        kv.at[pl.ds(ROWS, TILE)], kv.at[pl.ds(TILE + ROWS, TILE)], halo_s.at[1], halo_r.at[1],
        device_id=(sec, partner), device_id_type=MESH,
    )
    halo_l.start()
    halo_h.start()

    qs = dot(xn[...], wq[:, 0:D], 1, 0).astype(BF).astype(F32) * SCALE
    for b in range(BLK):
        for p in range(PAIRS):
            qb = qs[b * TILE : (b + 1) * TILE, p * TILE : (p + 1) * TILE]
            q2[b * PAIRS + p, 0:TILE, :] = (qb * m0).astype(BF)
            q2[b * PAIRS + p, TILE:, :] = (qb * m1).astype(BF)

    def forward(b):
        spot = place(b)
        here = dom * BLK + spot
        low = lax.rem(here + DOM * BLK - 1 + 2 * c, DOM * BLK)
        high = lax.rem(here + DOM * BLK + 1 - 2 * c, DOM * BLK)
        n1 = jnp.full((TILE, 2 * TILE), nbr[spot, 1], jnp.int32)
        n2 = jnp.full((TILE, 2 * TILE), nbr[spot, 2], jnp.int32)
        has_low = (n1 == low) | (n2 == low)
        has_high = (n1 == high) | (n2 == high)
        for p in range(PAIRS):
            keys = kv[b * TILE : b * TILE + KEYS, p * TILE : (p + 1) * TILE]
            s = dot(keys, q2[b * PAIRS + p], 1, 1)
            s = jnp.concatenate(
                [
                    jnp.where(has_low, s[0:TILE], -1e30),
                    s[TILE : 2 * TILE],
                    jnp.where(has_high, s[2 * TILE :], -1e30),
                ],
                axis=0,
            )
            top = jnp.max(s, axis=0, keepdims=True)
            e = jnp.exp(s - top)
            pr[b * PAIRS + p] = (e * (1.0 / jnp.sum(e, axis=0, keepdims=True))).astype(BF)

    def flip(e, h):
        kvT[h * D : (h + 1) * D, e * TILE : (e + 1) * TILE] = kv[
            e * TILE : (e + 1) * TILE, h * D : (h + 1) * D
        ].T

    forward(1)
    for e in range(1, 4):
        flip(e, 0)
    halo_h.wait_recv()
    flip(4, 0)
    forward(2)
    halo_l.wait_recv()
    flip(0, 0)
    forward(0)
    load_wo.wait()

    def prepare():
        for e in range(EXT // TILE):
            flip(e, 1)
        for b in range(BLK):
            cols = slice(b * TILE, (b + 1) * TILE)
            for p in range(PAIRS):
                o = dot(
                    kvT[D + p * TILE : D + (p + 1) * TILE, b * TILE : b * TILE + KEYS],
                    pr[b * PAIRS + p], 1, 0,
                )
                o = jnp.concatenate([o[0:HDIM, 0:TILE], o[HDIM:, TILE:]], axis=0)
                o = o.reshape(TILE // 16, 2, 8, TILE)
                for s in range(2):
                    attnT[s, p * HDIM : (p + 1) * HDIM, cols] = (
                        o[:, s].reshape(HDIM, TILE).astype(BF)
                    )
            t = xhat[b * TILE : (b + 1) * TILE, :].T.reshape(HALF // 8, 2, 8, TILE)
            for s in range(2):
                xnT[s, :, cols] = t[:, s].reshape(HALF, TILE).astype(BF)

    @pl.when(sec < SEC - 1)
    def _():
        prepare()

    def g_copy(b):
        return pltpu.make_async_remote_copy(
            gout.at[b], g_v.at[b], g_s.at[b], g_r.at[b],
            device_id=(before, dom), device_id_type=MESH,
        )

    send_l = pltpu.make_async_remote_copy(
        rim_lo, rim_l, rim_ss.at[0], rim_rs.at[0], device_id=(sec, left), device_id_type=MESH
    )
    send_h = pltpu.make_async_remote_copy(
        rim_hi, rim_r, rim_ss.at[1], rim_rs.at[1], device_id=(sec, partner), device_id_type=MESH
    )

    def step(b):
        @pl.when(sec == SEC - 1)
        def _():
            load_g[b].wait()

        @pl.when(sec < SEC - 1)
        def _():
            g_copy(b).wait_recv()

        da = dot(g_v[b], wo[...], 1, 1).astype(BF).astype(F32)
        for p in range(PAIRS):
            db = da[:, p * TILE : (p + 1) * TILE]
            da2[b * PAIRS + p, 0:TILE, :] = (db * m0).astype(BF)
            da2[b * PAIRS + p, TILE:, :] = (db * m1).astype(BF)
        for p in range(PAIRS):
            vals = kv[b * TILE : b * TILE + KEYS, D + p * TILE : D + (p + 1) * TILE]
            d2 = da2[b * PAIRS + p]
            pb = pr[b * PAIRS + p]
            dp = dot(vals, d2, 1, 1)
            pf = pb.astype(F32)
            delta = jnp.sum(dp * pf, axis=0, keepdims=True)
            ds = (pf * (dp - delta)).astype(BF)
            for term, off in ((dot(pb, d2, 1, 0), D), (dot(ds, q2[b * PAIRS + p], 1, 0), 0)):
                cols = slice(off + p * TILE, off + (p + 1) * TILE)
                for t in range(3):
                    rows = slice((b + t) * TILE, (b + t + 1) * TILE)
                    val = term[t * TILE : (t + 1) * TILE]
                    if b == 0 or t == 2:
                        acc[rows, cols] = val
                    else:
                        acc[rows, cols] = acc[rows, cols] + val
            dq = dot(kvT[p * TILE : (p + 1) * TILE, b * TILE : b * TILE + KEYS], ds, 1, 0)
            dq = jnp.concatenate([dq[0:HDIM, 0:TILE], dq[HDIM:, TILE:]], axis=0)
            dqkv[b * TILE : (b + 1) * TILE, p * TILE : (p + 1) * TILE] = (dq.T * SCALE).astype(BF)

    def close(b):
        dkv = acc[(b + 1) * TILE : (b + 2) * TILE, :]
        if b == 0:
            send_l.wait_recv()
            dkv = dkv + rim_l[...].astype(F32)
        if b == 2:
            send_h.wait_recv()
            dkv = dkv + rim_r[...].astype(F32)
        dqkv[b * TILE : (b + 1) * TILE, D:] = dkv.astype(BF)

    def finish(b):
        rows = pl.ds(b * TILE, TILE)
        dn = dot(dqkv[rows, :], wq[...], 1, 1)
        xh = xhat[rows, :]
        inv = inv_v[rows, 0:1]
        ln = inv * (
            dn
            - jnp.mean(dn, axis=-1, keepdims=True)
            - xh * jnp.mean(dn * xh, axis=-1, keepdims=True)
        )
        gout[b] = (g_v[b].astype(F32) + ln).astype(BF)

    def store(b):
        return pltpu.make_async_copy(gout.at[b], gout_hbm.at[place(b)], out_sem.at[b])

    def pass_on(b):
        close(b)
        finish(b)
        g_copy(b).start()
        store(b).start()

    def c_copy(j):
        send, recv, _, ss, rs = cores[j]
        return pltpu.make_async_remote_copy(
            send, recv, ss, rs, device_id=(sec, partner), device_id_type=MESH
        )

    def axis_copy(j, stage, o):
        first = CHUNKS[j][2]
        axis = first if stage == 0 else ("z" if first == "y" else "y")
        send, recv, _, ss, rs = (firsts if stage == 0 else seconds)[j]
        to = y_dev(o) if axis == "y" else z_dev(o)
        return pltpu.make_async_remote_copy(
            send.at[o - 1], recv.at[o - 1], ss.at[o - 1], rs.at[o - 1],
            device_id=(sec, to), device_id_type=MESH,
        )

    def multiply(j, who):
        off, width, _ = CHUNKS[j]
        if off == 3 * D:
            return dot(attnT[who], g_v[...].reshape(ROWS, D), 1, 0)
        return dot(xnT[who], dqkv[:, off : off + width], 1, 0)

    def open_sum(j):
        cores[j][0][...] = multiply(j, 1 - c).astype(BF)
        c_copy(j).start()
        cores[j][2][...] = multiply(j, c).reshape(NY, NZ, 8, CHUNKS[j][1])

    def first_sum(j):
        width = CHUNKS[j][1]
        c_copy(j).wait_recv()
        held = cores[j][2]
        held[...] = held[...] + cores[j][1][...].astype(F32).reshape(NY, NZ, 8, width)
        send = firsts[j][0]
        if CHUNKS[j][2] == "y":
            for o in range(1, NY):
                send[o - 1] = held[lax.rem(y + o, NY)].reshape(NZ * 8, width).astype(BF)
                axis_copy(j, 0, o).start()
        else:
            for o in range(1, NZ):
                send[o - 1] = held[:, lax.rem(z + o, NZ)].reshape(NY * 8, width).astype(BF)
                axis_copy(j, 0, o).start()

    def fold(piece):
        width = piece.shape[1] // 2
        return jnp.concatenate([piece[:, 0:width], piece[:, width:]], axis=0)

    def second_sum(j):
        width = CHUNKS[j][1]
        held = cores[j][2]
        if CHUNKS[j][2] == "y":
            mine, n1, n2, me = held[y], NY, NZ, z
        else:
            mine, n1, n2, me = held[:, z], NZ, NY, y
        for o in range(1, n1):
            axis_copy(j, 0, o).wait_recv()
            mine = mine + firsts[j][1][o - 1].astype(F32).reshape(n2, 8, width)
        part = firsts[j][2]
        part[...] = mine
        for o in range(1, n2):
            seconds[j][0][o - 1] = fold(part[lax.rem(me + o, n2)]).astype(BF)
            axis_copy(j, 1, o).start()

    def end_sum(j):
        off, width, first = CHUNKS[j]
        me, n2 = (z, NZ) if first == "y" else (y, NY)
        total = fold(firsts[j][2][me])
        for o in range(1, n2):
            axis_copy(j, 1, o).wait_recv()
            total = total + seconds[j][1][o - 1].astype(F32)
        total = jnp.concatenate([total[0:8], total[8:16]], axis=1)
        if off == 3 * D:
            dwo_ref[...] = total
        else:
            dwq_ref[:, off : off + width] = total

    step(0)
    rim_lo[...] = acc[0:TILE, :].astype(BF)
    send_l.start()
    step(1)

    @pl.when(sec > 0)
    def _():
        pass_on(0)

    step(2)
    rim_hi[...] = acc[EXT - TILE :, :].astype(BF)
    send_h.start()

    @pl.when(sec > 0)
    def _():
        pass_on(1)
        pass_on(2)

        @pl.when(sec == SEC - 1)
        def _():
            prepare()

        for j in range(len(CHUNKS)):
            open_sum(j)
        for j in range(len(CHUNKS)):
            first_sum(j)

    @pl.when(sec == 0)
    def _():
        open_sum(0)
        open_sum(1)
        close(0)
        close(1)
        first_sum(0)
        first_sum(1)
        close(2)
        for j in range(2, len(CHUNKS)):
            open_sum(j)
        for j in range(2, len(CHUNKS)):
            first_sum(j)
        for b in range(BLK):
            finish(b)
            store(b).start()

    for j in range(len(CHUNKS)):
        second_sum(j)
    for j in range(len(CHUNKS)):
        end_sum(j)

    halo_l.wait_send()
    halo_h.wait_send()
    send_l.wait_send()
    send_h.wait_send()

    @pl.when(sec > 0)
    def _():
        for b in range(BLK):
            g_copy(b).wait_send()

    for j in range(len(CHUNKS)):
        c_copy(j).wait_send()
        for o in range(1, NY if CHUNKS[j][2] == "y" else NZ):
            axis_copy(j, 0, o).wait_send()
        for o in range(1, NZ if CHUNKS[j][2] == "y" else NY):
            axis_copy(j, 1, o).wait_send()
    for b in range(BLK):
        store(b).wait()


def copy_body(a, b, c, a_out, b_out, c_out, sem):
    copies = [
        pltpu.make_async_copy(src, dst, sem.at[i])
        for i, (src, dst) in enumerate(((a, a_out), (b, b_out), (c, c_out)))
    ]
    for copy in copies:
        copy.start()
    for copy in copies:
        copy.wait()


def local(layer_inputs, top_grad, w_qkv, w_out, neighbours):
    vm = pltpu.VMEM
    sem = pltpu.SemaphoreType.DMA
    anyspec = pl.BlockSpec(memory_space=pl.ANY)
    vspec = pl.BlockSpec(memory_space=pltpu.VMEM)
    outs = (
        jax.ShapeDtypeStruct((BLK, TILE, D), BF),
        jax.ShapeDtypeStruct((D // DOM, 3 * D), F32),
        jax.ShapeDtypeStruct((D // DOM, D), F32),
    )
    cores, firsts, seconds = [], [], []
    for _, width, first in CHUNKS:
        n1, n2 = (NY, NZ) if first == "y" else (NZ, NY)
        cores.append(
            (vm((HALF, width), BF), vm((HALF, width), BF), vm((NY, NZ, 8, width), F32), sem(()), sem(()))
        )
        firsts.append(
            (
                vm((n1 - 1, n2 * 8, width), BF), vm((n1 - 1, n2 * 8, width), BF),
                vm((n2, 8, width), F32), sem((n1 - 1,)), sem((n1 - 1,)),
            )
        )
        seconds.append(
            (
                vm((n2 - 1, 16, width // 2), BF), vm((n2 - 1, 16, width // 2), BF),
                vm((8, 128), F32), sem((n2 - 1,)), sem((n2 - 1,)),
            )
        )
    results = pl.pallas_call(
        body,
        out_shape=outs,
        in_specs=[pl.BlockSpec(memory_space=pltpu.SMEM)] + [anyspec] * 4,
        out_specs=(anyspec, vspec, vspec),
        scratch_shapes=[
            vm((BLK, TILE, D), BF),
            vm((D, 3 * D), BF),
            vm((D, D), BF),
            vm((BLK, TILE, D), BF),
            vm((ROWS, D), F32),
            vm((ROWS, TILE), F32),
            vm((ROWS, D), BF),
            vm((NC, HALF, ROWS), BF),
            vm((BLK * PAIRS, 2 * TILE, TILE), BF),
            vm((EXT, 2 * D), BF),
            vm((2 * D, EXT), BF),
            vm((BLK * PAIRS, KEYS, 2 * TILE), BF),
            vm((NC, HALF, ROWS), BF),
            vm((BLK * PAIRS, 2 * TILE, TILE), BF),
            vm((EXT, 2 * D), F32),
            vm((TILE, 2 * D), BF),
            vm((TILE, 2 * D), BF),
            vm((TILE, 2 * D), BF),
            vm((TILE, 2 * D), BF),
            vm((ROWS, 3 * D), BF),
            vm((BLK, TILE, D), BF),
            sem((2 * BLK + 2,)), sem((BLK,)),
            sem((2,)), sem((2,)), sem((2,)), sem((2,)), sem((BLK,)), sem((BLK,)),
            cores, firsts, seconds,
        ],
        compiler_params=pltpu.CompilerParams(
            collective_id=0, has_side_effects=True, vmem_limit_bytes=60 << 20
        ),
        name="layer_backward",
    )(
        neighbours,
        layer_inputs.reshape(BLK, TILE, D),
        top_grad.reshape(BLK, TILE, D),
        w_qkv.reshape(D, 3 * D),
        w_out.reshape(D, D),
    )
    gin, dwq, dwo = pl.pallas_call(
        copy_body,
        out_shape=outs,
        in_specs=[anyspec] * 3,
        out_specs=(anyspec,) * 3,
        scratch_shapes=[sem((3,))],
        name="results",
    )(*results)
    return (gin.reshape(1, 1, ROWS, D), dwq[None], dwo[None])


def solution(mesh):
    placed = (
        P("section", None, "dom", None),
        P(None, "dom", None),
        P("section", None, None),
        P("section", None, None),
        P("dom", None),
    )
    return jax.shard_map(
        local,
        mesh=mesh,
        in_specs=placed,
        out_specs=(
            P("section", None, "dom", None),
            P("section", "dom", None),
            P("section", "dom", None),
        ),
        check_vma=False,
    )
```

```python
import jax
import jax.numpy as jnp
from jax import lax
from jax.experimental import pallas as pl
from jax.experimental.pallas import tpu as pltpu
from jax.sharding import PartitionSpec as P

SEC = 4
NY, NZ, NC = 4, 8, 2
DOM = NY * NZ * NC
D = 512
HEADS = 8
HDIM = D // HEADS
PAIRS = HEADS // 2
TILE = 128
BLK = 3
KEYS = 3 * TILE
ROWS = BLK * TILE
EXT = ROWS + 2 * TILE
HALF = NY * NZ * 8
SCALE = 1.0 / HDIM**0.5
BF = jnp.bfloat16
F32 = jnp.float32
MESH = pl.DeviceIdType.MESH
CHUNKS = ((1536, 512, "y"), (0, 512, "y"), (512, 512, "y"), (1024, 256, "y"), (1280, 256, "z"))


def dot(a, b, ca, cb):
    return lax.dot_general(a, b, (((ca,), (cb,)), ((), ())), preferred_element_type=F32)


def body(
    nbr, x_hbm, g_hbm, wq_hbm, wo_hbm, gout_hbm, dwq_ref, dwo_ref,
    x_v, wq, wo, g_v, xhat, inv_v, xn, xnT, q2, kv, kvT, pr, attnT, da2, acc,
    rim_out, rim_in, accb, dqkv, gout,
    in_sem, out_sem, halo_s, halo_r, rim_ss, rim_rs, g_s, g_r, cores, firsts, seconds,
):
    sec = lax.axis_index("section")
    dom = lax.axis_index("dom")
    y = lax.div(dom, NZ * NC)
    z = lax.rem(lax.div(dom, NC), NZ)
    c = lax.rem(dom, NC)
    other = lax.rem(dom + DOM - 1 + 2 * c, DOM)
    partner = dom + 1 - 2 * c
    before = lax.rem(sec + SEC - 1, SEC)
    after = lax.rem(sec + 1, SEC)

    def place(i):
        return i + (1 - c) * (2 - 2 * i)

    def y_dev(o):
        return lax.rem(y + o, NY) * (NZ * NC) + z * NC + c

    def z_dev(o):
        return y * (NZ * NC) + lax.rem(z + o, NZ) * NC + c

    load_x = [pltpu.make_async_copy(x_hbm.at[place(i)], x_v.at[i], in_sem.at[i]) for i in range(BLK)]
    load_g = [
        pltpu.make_async_copy(g_hbm.at[place(i)], g_v.at[i], in_sem.at[BLK + i]) for i in range(BLK)
    ]
    load_wq = pltpu.make_async_copy(wq_hbm, wq, in_sem.at[2 * BLK])
    load_wo = pltpu.make_async_copy(wo_hbm, wo, in_sem.at[2 * BLK + 1])
    for copy in load_x:
        copy.start()
    load_wq.start()
    load_wo.start()

    @pl.when(sec == SEC - 1)
    def _():
        for copy in load_g:
            copy.start()

    barrier = pltpu.get_barrier_semaphore()
    peers = [(sec, other), (sec, partner), (before, dom), (after, dom)]
    peers += [(sec, y_dev(o)) for o in range(1, NY)]
    peers += [(sec, z_dev(o)) for o in range(1, NZ)]
    for peer in peers:
        pl.semaphore_signal(barrier, inc=1, device_id=peer, device_id_type=MESH)

    lane = lax.broadcasted_iota(jnp.int32, (1, TILE), 1)
    m0 = jnp.where(lane < HDIM, 1.0, 0.0)
    m1 = 1.0 - m0

    for b in range(BLK):
        load_x[b].wait()
        rows = pl.ds(b * TILE, TILE)
        own = pl.ds((b + 1) * TILE, TILE)
        xf = x_v[b].astype(F32)
        cen = xf - jnp.mean(xf, axis=-1, keepdims=True)
        inv = lax.rsqrt(jnp.mean(cen * cen, axis=-1, keepdims=True) + 1e-05)
        xh = cen * inv
        xhat[rows, :] = xh
        inv_v[rows, :] = jnp.broadcast_to(inv, (TILE, TILE))
        xn[own, :] = xh.astype(BF)

    load_wq.wait()
    for h in range(2):
        part = dot(xn[TILE : TILE + ROWS, :], wq[:, (1 + h) * D : (2 + h) * D], 1, 0)
        kv[TILE : TILE + ROWS, h * D : (h + 1) * D] = part.astype(BF)
    pl.semaphore_wait(barrier, len(peers))
    def halo(ref, side):
        sem, to = (0, partner) if side == 0 else (1, other)
        source, target = (TILE, 0) if side == 0 else (ROWS, TILE + ROWS)
        if ref is xn:
            sem = sem + 2
        return pltpu.make_async_remote_copy(
            ref.at[pl.ds(source, TILE)], ref.at[pl.ds(target, TILE)],
            halo_s.at[sem], halo_r.at[sem], device_id=(sec, to), device_id_type=MESH,
        )

    halo(kv, 1).start()
    halo(kv, 0).start()
    halo(xn, 0).start()
    halo(xn, 1).start()

    qs = dot(xn[TILE : TILE + ROWS, :], wq[:, 0:D], 1, 0).astype(BF).astype(F32) * SCALE
    for b in range(BLK):
        for p in range(PAIRS):
            qb = qs[b * TILE : (b + 1) * TILE, p * TILE : (p + 1) * TILE]
            q2[b * PAIRS + p, 0:TILE, :] = (qb * m0).astype(BF)
            q2[b * PAIRS + p, TILE:, :] = (qb * m1).astype(BF)

    def forward(b):
        spot = place(b)
        here = dom * BLK + spot
        low = lax.rem(here + DOM * BLK + 1 - 2 * c, DOM * BLK)
        high = lax.rem(here + DOM * BLK - 1 + 2 * c, DOM * BLK)
        n1 = jnp.full((TILE, 2 * TILE), nbr[spot, 1], jnp.int32)
        n2 = jnp.full((TILE, 2 * TILE), nbr[spot, 2], jnp.int32)
        has_low = (n1 == low) | (n2 == low)
        has_high = (n1 == high) | (n2 == high)
        for p in range(PAIRS):
            keys = kv[b * TILE : b * TILE + KEYS, p * TILE : (p + 1) * TILE]
            s = dot(keys, q2[b * PAIRS + p], 1, 1)
            s = jnp.concatenate(
                [
                    jnp.where(has_low, s[0:TILE], -1e30),
                    s[TILE : 2 * TILE],
                    jnp.where(has_high, s[2 * TILE :], -1e30),
                ],
                axis=0,
            )
            top = jnp.max(s, axis=0, keepdims=True)
            e = jnp.exp(s - top)
            pr[b * PAIRS + p] = (e * (1.0 / jnp.sum(e, axis=0, keepdims=True))).astype(BF)

    def flip(e, h):
        kvT[h * D : (h + 1) * D, e * TILE : (e + 1) * TILE] = kv[
            e * TILE : (e + 1) * TILE, h * D : (h + 1) * D
        ].T

    def forward_last():
        halo(kv, 1).wait_recv()
        flip(4, 0)
        forward(2)

    forward(1)
    for e in range(1, 4):
        flip(e, 0)
    halo(kv, 0).wait_recv()
    flip(0, 0)
    forward(0)
    load_wo.wait()

    def prepare():
        halo(xn, 0).wait_recv()
        halo(xn, 1).wait_recv()
        for e in range(EXT // TILE):
            flip(e, 1)
            cols = slice(e * TILE, (e + 1) * TILE)
            t = xn[cols, :].astype(F32).T.reshape(HALF // 8, 2, 8, TILE)
            for s in range(2):
                xnT[s, :, cols] = t[:, s].reshape(HALF, TILE).astype(BF)
        for b in range(BLK):
            cols = slice(b * TILE, (b + 1) * TILE)
            for p in range(PAIRS):
                o = dot(
                    kvT[D + p * TILE : D + (p + 1) * TILE, b * TILE : b * TILE + KEYS],
                    pr[b * PAIRS + p], 1, 0,
                )
                o = jnp.concatenate([o[0:HDIM, 0:TILE], o[HDIM:, TILE:]], axis=0)
                o = o.reshape(TILE // 16, 2, 8, TILE)
                for s in range(2):
                    attnT[s, p * HDIM : (p + 1) * HDIM, cols] = (
                        o[:, s].reshape(HDIM, TILE).astype(BF)
                    )

    @pl.when(sec < SEC - 1)
    def _():
        forward_last()
        prepare()

    def g_copy(b):
        return pltpu.make_async_remote_copy(
            gout.at[b], g_v.at[b], g_s.at[b], g_r.at[b],
            device_id=(before, dom), device_id_type=MESH,
        )

    def rim(side, h):
        return pltpu.make_async_remote_copy(
            rim_out.at[side, h], rim_in.at[side, h], rim_ss.at[side, h], rim_rs.at[side, h],
            device_id=(sec, partner if side == 0 else other), device_id_type=MESH,
        )

    def step(b):
        @pl.when(sec == SEC - 1)
        def _():
            load_g[b].wait()

        @pl.when(sec < SEC - 1)
        def _():
            g_copy(b).wait_recv()

        da = dot(g_v[b], wo[...], 1, 1).astype(BF).astype(F32)
        for p in range(PAIRS):
            db = da[:, p * TILE : (p + 1) * TILE]
            da2[b * PAIRS + p, 0:TILE, :] = (db * m0).astype(BF)
            da2[b * PAIRS + p, TILE:, :] = (db * m1).astype(BF)
        for p in range(PAIRS):
            vals = kv[b * TILE : b * TILE + KEYS, D + p * TILE : D + (p + 1) * TILE]
            d2 = da2[b * PAIRS + p]
            pb = pr[b * PAIRS + p]
            dp = dot(vals, d2, 1, 1)
            pf = pb.astype(F32)
            delta = jnp.sum(dp * pf, axis=0, keepdims=True)
            ds = (pf * (dp - delta)).astype(BF)
            for term, off in ((dot(pb, d2, 1, 0), D), (dot(ds, q2[b * PAIRS + p], 1, 0), 0)):
                cols = slice(off + p * TILE, off + (p + 1) * TILE)
                for t in range(3):
                    rows = slice((b + t) * TILE, (b + t + 1) * TILE)
                    val = term[t * TILE : (t + 1) * TILE]
                    if b == 0 or t == 2:
                        acc[rows, cols] = val
                    else:
                        acc[rows, cols] = acc[rows, cols] + val
            dq = dot(kvT[p * TILE : (p + 1) * TILE, b * TILE : b * TILE + KEYS], ds, 1, 0)
            dq = jnp.concatenate([dq[0:HDIM, 0:TILE], dq[HDIM:, TILE:]], axis=0)
            dqkv[b * TILE : (b + 1) * TILE, p * TILE : (p + 1) * TILE] = (dq.T * SCALE).astype(BF)
            if b != 1 and p % 2 == 1:
                side, h = b // 2, p // 2
                rows = slice(side * (EXT - TILE), side * (EXT - TILE) + TILE)
                for off in range(2):
                    start = off * D + h * (D // 2)
                    rim_out[side, h, :, off * (D // 2) : (off + 1) * (D // 2)] = acc[
                        rows, start : start + D // 2
                    ].astype(BF)
                rim(side, h).start()

    def close(b):
        dkv = acc[(b + 1) * TILE : (b + 2) * TILE, :]
        if b != 1:
            side = b // 2
            rim(side, 0).wait_recv()
            rim(side, 1).wait_recv()
            terms = [
                rim_in[side, h, :, off * (D // 2) : (off + 1) * (D // 2)].astype(F32)
                for off in range(2)
                for h in range(2)
            ]
            dkv = dkv + jnp.concatenate(terms, axis=1)
        dqkv[b * TILE : (b + 1) * TILE, D:] = dkv.astype(BF)

    def finish(b):
        rows = pl.ds(b * TILE, TILE)
        dn = dot(dqkv[rows, :], wq[...], 1, 1)
        xh = xhat[rows, :]
        inv = inv_v[rows, 0:1]
        ln = inv * (
            dn
            - jnp.mean(dn, axis=-1, keepdims=True)
            - xh * jnp.mean(dn * xh, axis=-1, keepdims=True)
        )
        gout[b] = (g_v[b].astype(F32) + ln).astype(BF)

    def store(b):
        return pltpu.make_async_copy(gout.at[b], gout_hbm.at[place(b)], out_sem.at[b])

    def pass_on(b):
        close(b)
        finish(b)
        g_copy(b).start()
        store(b).start()

    def c_copy(j):
        send, recv, _, ss, rs = cores[j]
        return pltpu.make_async_remote_copy(
            send, recv, ss, rs, device_id=(sec, partner), device_id_type=MESH
        )

    def axis_copy(j, stage, o):
        first = CHUNKS[j][2]
        axis = first if stage == 0 else ("z" if first == "y" else "y")
        refs = (firsts if stage == 0 else seconds)[j]
        send, recv, ss, rs = refs[0], refs[1], refs[-2], refs[-1]
        to = y_dev(o) if axis == "y" else z_dev(o)
        return pltpu.make_async_remote_copy(
            send.at[o - 1], recv.at[o - 1], ss.at[o - 1], rs.at[o - 1],
            device_id=(sec, to), device_id_type=MESH,
        )

    def multiply(j, who):
        off, width, _ = CHUNKS[j]
        if off == 3 * D:
            return dot(attnT[who], g_v[...].reshape(ROWS, D), 1, 0)
        if off == 0:
            return dot(xnT[who, :, TILE : TILE + ROWS], dqkv[:, 0:D], 1, 0)
        return dot(xnT[who], accb[:, off - D : off - D + width], 1, 0)

    def open_sum(j):
        cores[j][0][...] = multiply(j, 1 - c).astype(BF)
        c_copy(j).start()
        cores[j][2][...] = multiply(j, c).reshape(NY, NZ, 8, CHUNKS[j][1])

    def first_sum(j):
        width = CHUNKS[j][1]
        c_copy(j).wait_recv()
        held = cores[j][2]
        held[...] = held[...] + cores[j][1][...].astype(F32).reshape(NY, NZ, 8, width)
        send = firsts[j][0]
        if CHUNKS[j][2] == "y":
            for o in range(1, NY):
                send[o - 1] = held[lax.rem(y + o, NY)].reshape(NZ * 8, width).astype(BF)
                axis_copy(j, 0, o).start()
        else:
            for o in range(1, NZ):
                send[o - 1] = held[:, lax.rem(z + o, NZ)].reshape(NY * 8, width).astype(BF)
                axis_copy(j, 0, o).start()

    def fold(piece):
        width = piece.shape[1] // 2
        return jnp.concatenate([piece[:, 0:width], piece[:, width:]], axis=0)

    def second_sum(j):
        width = CHUNKS[j][1]
        held = cores[j][2]
        if CHUNKS[j][2] == "y":
            mine, n1, n2, me = held[y], NY, NZ, z
        else:
            mine, n1, n2, me = held[:, z], NZ, NY, y
        for o in range(1, n1):
            axis_copy(j, 0, o).wait_recv()
            mine = mine + firsts[j][1][o - 1].astype(F32).reshape(n2, 8, width)
        part = firsts[j][2]
        part[...] = mine
        for o in range(1, n2):
            seconds[j][0][o - 1] = fold(part[lax.rem(me + o, n2)]).astype(BF)
            axis_copy(j, 1, o).start()

    def end_sum(j):
        off, width, first = CHUNKS[j]
        me, n2 = (z, NZ) if first == "y" else (y, NY)
        total = fold(firsts[j][2][me])
        for o in range(1, n2):
            axis_copy(j, 1, o).wait_recv()
            total = total + seconds[j][1][o - 1].astype(F32)
        total = jnp.concatenate([total[0:8], total[8:16]], axis=1)
        if off == 3 * D:
            dwo_ref[...] = total
        else:
            dwq_ref[:, off : off + width] = total

    step(0)
    step(1)

    @pl.when(sec > 0)
    def _():
        pass_on(0)

    @pl.when(sec == SEC - 1)
    def _():
        forward_last()

    step(2)

    @pl.when(sec > 0)
    def _():
        pass_on(1)
        pass_on(2)

        @pl.when(sec == SEC - 1)
        def _():
            prepare()

    for h in range(4):
        cols = slice(h * (D // 2), (h + 1) * (D // 2))
        accb[:, cols] = acc[:, cols].astype(BF)
    for j in range(len(CHUNKS)):
        open_sum(j)
    for j in range(len(CHUNKS)):
        first_sum(j)

    @pl.when(sec == 0)
    def _():
        for b in range(BLK):
            close(b)
            finish(b)
            store(b).start()

    for j in range(len(CHUNKS)):
        second_sum(j)
    for j in range(len(CHUNKS)):
        end_sum(j)

    for side in range(2):
        halo(kv, side).wait_send()
        halo(xn, side).wait_send()
        rim(side, 0).wait_send()
        rim(side, 1).wait_send()

    @pl.when(sec > 0)
    def _():
        for b in range(BLK):
            g_copy(b).wait_send()

    for j in range(len(CHUNKS)):
        c_copy(j).wait_send()
        for o in range(1, NY if CHUNKS[j][2] == "y" else NZ):
            axis_copy(j, 0, o).wait_send()
        for o in range(1, NZ if CHUNKS[j][2] == "y" else NY):
            axis_copy(j, 1, o).wait_send()
    for b in range(BLK):
        store(b).wait()


def copy_body(a, b, c, a_out, b_out, c_out):
    a_out[...] = a[...]
    b_out[...] = b[...]
    c_out[...] = c[...]


def local(layer_inputs, top_grad, w_qkv, w_out, neighbours):
    vm = pltpu.VMEM
    sem = pltpu.SemaphoreType.DMA
    anyspec = pl.BlockSpec(memory_space=pl.ANY)
    vspec = pl.BlockSpec(memory_space=pltpu.VMEM)
    outs = (
        jax.ShapeDtypeStruct((BLK, TILE, D), BF),
        jax.ShapeDtypeStruct((D // DOM, 3 * D), F32),
        jax.ShapeDtypeStruct((D // DOM, D), F32),
    )
    cores, firsts, seconds = [], [], []
    for _, width, first in CHUNKS:
        n1, n2 = (NY, NZ) if first == "y" else (NZ, NY)
        cores.append(
            (vm((HALF, width), BF), vm((HALF, width), BF), vm((NY, NZ, 8, width), F32), sem(()), sem(()))
        )
        firsts.append(
            (
                vm((n1 - 1, n2 * 8, width), BF), vm((n1 - 1, n2 * 8, width), BF),
                vm((n2, 8, width), F32), sem((n1 - 1,)), sem((n1 - 1,)),
            )
        )
        seconds.append(
            (
                vm((n2 - 1, 16, width // 2), BF), vm((n2 - 1, 16, width // 2), BF),
                sem((n2 - 1,)), sem((n2 - 1,)),
            )
        )
    results = pl.pallas_call(
        body,
        out_shape=outs,
        in_specs=[pl.BlockSpec(memory_space=pltpu.SMEM)] + [anyspec] * 4,
        out_specs=(anyspec, vspec, vspec),
        scratch_shapes=[
            vm((BLK, TILE, D), BF),
            vm((D, 3 * D), BF),
            vm((D, D), BF),
            vm((BLK, TILE, D), BF),
            vm((ROWS, D), F32),
            vm((ROWS, TILE), F32),
            vm((EXT, D), BF),
            vm((NC, HALF, EXT), BF),
            vm((BLK * PAIRS, 2 * TILE, TILE), BF),
            vm((EXT, 2 * D), BF),
            vm((2 * D, EXT), BF),
            vm((BLK * PAIRS, KEYS, 2 * TILE), BF),
            vm((NC, HALF, ROWS), BF),
            vm((BLK * PAIRS, 2 * TILE, TILE), BF),
            vm((EXT, 2 * D), F32),
            vm((2, 2, TILE, D), BF),
            vm((2, 2, TILE, D), BF),
            vm((EXT, 2 * D), BF),
            vm((ROWS, 3 * D), BF),
            vm((BLK, TILE, D), BF),
            sem((2 * BLK + 2,)), sem((BLK,)),
            sem((4,)), sem((4,)), sem((2, 2)), sem((2, 2)), sem((BLK,)), sem((BLK,)),
            cores, firsts, seconds,
        ],
        compiler_params=pltpu.CompilerParams(
            collective_id=0, has_side_effects=True, vmem_limit_bytes=60 << 20
        ),
        name="layer_backward",
    )(
        neighbours,
        layer_inputs.reshape(BLK, TILE, D),
        top_grad.reshape(BLK, TILE, D),
        w_qkv.reshape(D, 3 * D),
        w_out.reshape(D, D),
    )
    gin, dwq, dwo = pl.pallas_call(
        copy_body,
        out_shape=outs,
        in_specs=[vspec] * 3,
        out_specs=(vspec,) * 3,
        name="results",
    )(*results)
    return (gin.reshape(1, 1, ROWS, D), dwq[None], dwo[None])


def solution(mesh):
    placed = (
        P("section", None, "dom", None),
        P(None, "dom", None),
        P("section", None, None),
        P("section", None, None),
        P("dom", None),
    )
    return jax.shard_map(
        local,
        mesh=mesh,
        in_specs=placed,
        out_specs=(
            P("section", None, "dom", None),
            P("section", "dom", None),
            P("section", "dom", None),
        ),
        check_vma=False,
    )
```

```python
import jax
import jax.numpy as jnp
from jax import lax
from jax.experimental import pallas as pl
from jax.experimental.pallas import tpu as pltpu
from jax.sharding import PartitionSpec as P

SEC = 4
NY, NZ, NC = 4, 8, 2
DOM = NY * NZ * NC
D = 512
HEADS = 8
HDIM = D // HEADS
PAIRS = HEADS // 2
TILE = 128
BLK = 3
KEYS = 3 * TILE
ROWS = BLK * TILE
EXT = ROWS + 2 * TILE
HALF = NY * NZ * 8
SCALE = 1.0 / HDIM**0.5
BF = jnp.bfloat16
F32 = jnp.float32
MESH = pl.DeviceIdType.MESH
CHUNKS = ((1536, 512, "y"), (1024, 512, "z"), (0, 512, "y"), (512, 512, "y"))


def dot(a, b, ca, cb):
    return lax.dot_general(a, b, (((ca,), (cb,)), ((), ())), preferred_element_type=F32)


def body(
    nbr, x_hbm, g_hbm, wq_hbm, wo_hbm, gout_hbm, dwq_ref, dwo_ref,
    x_v, wq, wo, g_v, xhat, inv_v, xn, xnT, q2, kv, kvT, pr, attnT, da2, acc,
    rim_out, rim_in, accb, dsc, dqkv, gout,
    in_sem, out_sem, halo_s, halo_r, rim_ss, rim_rs, g_s, g_r, cores, firsts, seconds,
):
    sec = lax.axis_index("section")
    dom = lax.axis_index("dom")
    y = lax.div(dom, NZ * NC)
    z = lax.rem(lax.div(dom, NC), NZ)
    c = lax.rem(dom, NC)
    other = lax.rem(dom + DOM - 1 + 2 * c, DOM)
    partner = dom + 1 - 2 * c
    before = lax.rem(sec + SEC - 1, SEC)
    after = lax.rem(sec + 1, SEC)

    def place(i):
        return i + (1 - c) * (2 - 2 * i)

    def y_dev(o):
        return lax.rem(y + o, NY) * (NZ * NC) + z * NC + c

    def z_dev(o):
        return y * (NZ * NC) + lax.rem(z + o, NZ) * NC + c

    load_x = [pltpu.make_async_copy(x_hbm.at[place(i)], x_v.at[i], in_sem.at[i]) for i in range(BLK)]
    load_g = [
        pltpu.make_async_copy(g_hbm.at[place(i)], g_v.at[i], in_sem.at[BLK + i]) for i in range(BLK)
    ]
    load_wq = pltpu.make_async_copy(wq_hbm, wq, in_sem.at[2 * BLK])
    load_wo = pltpu.make_async_copy(wo_hbm, wo, in_sem.at[2 * BLK + 1])
    for copy in load_x:
        copy.start()
    load_wq.start()
    load_wo.start()

    @pl.when(sec == SEC - 1)
    def _():
        for copy in load_g:
            copy.start()

    barrier = pltpu.get_barrier_semaphore()
    peers = [(sec, other), (sec, partner), (before, dom), (after, dom)]
    peers += [(sec, y_dev(o)) for o in range(1, NY)]
    peers += [(sec, z_dev(o)) for o in range(1, NZ)]
    for peer in peers:
        pl.semaphore_signal(barrier, inc=1, device_id=peer, device_id_type=MESH)

    lane = lax.broadcasted_iota(jnp.int32, (1, TILE), 1)
    m0 = jnp.where(lane < HDIM, 1.0, 0.0)
    m1 = 1.0 - m0

    for b in range(BLK):
        load_x[b].wait()
        rows = pl.ds(b * TILE, TILE)
        own = pl.ds((b + 1) * TILE, TILE)
        xf = x_v[b].astype(F32)
        cen = xf - jnp.mean(xf, axis=-1, keepdims=True)
        inv = lax.rsqrt(jnp.mean(cen * cen, axis=-1, keepdims=True) + 1e-05)
        xh = cen * inv
        xhat[rows, :] = xh
        inv_v[rows, :] = jnp.broadcast_to(inv, (TILE, TILE))
        xn[own, :] = xh.astype(BF)

    load_wq.wait()
    for h in range(2):
        part = dot(xn[TILE : TILE + ROWS, :], wq[:, (1 + h) * D : (2 + h) * D], 1, 0)
        kv[TILE : TILE + ROWS, h * D : (h + 1) * D] = part.astype(BF)
    pl.semaphore_wait(barrier, len(peers))
    def halo(ref, side):
        sem, to = (0, partner) if side == 0 else (1, other)
        source, target = (TILE, 0) if side == 0 else (ROWS, TILE + ROWS)
        if ref is xn:
            sem = sem + 2
        return pltpu.make_async_remote_copy(
            ref.at[pl.ds(source, TILE)], ref.at[pl.ds(target, TILE)],
            halo_s.at[sem], halo_r.at[sem], device_id=(sec, to), device_id_type=MESH,
        )

    halo(kv, 1).start()
    halo(kv, 0).start()
    halo(xn, 0).start()
    halo(xn, 1).start()

    qs = dot(xn[TILE : TILE + ROWS, :], wq[:, 0:D], 1, 0).astype(BF).astype(F32) * SCALE
    for b in range(BLK):
        for p in range(PAIRS):
            qb = qs[b * TILE : (b + 1) * TILE, p * TILE : (p + 1) * TILE]
            q2[b * PAIRS + p, 0:TILE, :] = (qb * m0).astype(BF)
            q2[b * PAIRS + p, TILE:, :] = (qb * m1).astype(BF)

    def forward(b):
        spot = place(b)
        here = dom * BLK + spot
        low = lax.rem(here + DOM * BLK + 1 - 2 * c, DOM * BLK)
        high = lax.rem(here + DOM * BLK - 1 + 2 * c, DOM * BLK)
        n1 = jnp.full((TILE, 2 * TILE), nbr[spot, 1], jnp.int32)
        n2 = jnp.full((TILE, 2 * TILE), nbr[spot, 2], jnp.int32)
        has_low = (n1 == low) | (n2 == low)
        has_high = (n1 == high) | (n2 == high)
        for p in range(PAIRS):
            keys = kv[b * TILE : b * TILE + KEYS, p * TILE : (p + 1) * TILE]
            s = dot(keys, q2[b * PAIRS + p], 1, 1)
            s = jnp.concatenate(
                [
                    jnp.where(has_low, s[0:TILE], -1e30),
                    s[TILE : 2 * TILE],
                    jnp.where(has_high, s[2 * TILE :], -1e30),
                ],
                axis=0,
            )
            top = jnp.max(s, axis=0, keepdims=True)
            e = jnp.exp(s - top)
            pr[b * PAIRS + p] = (e * (1.0 / jnp.sum(e, axis=0, keepdims=True))).astype(BF)

    def flip(e, h):
        kvT[h * D : (h + 1) * D, e * TILE : (e + 1) * TILE] = kv[
            e * TILE : (e + 1) * TILE, h * D : (h + 1) * D
        ].T

    def forward_last():
        halo(kv, 1).wait_recv()
        flip(4, 0)
        forward(2)

    forward(1)
    for e in range(1, 4):
        flip(e, 0)
    halo(kv, 0).wait_recv()
    flip(0, 0)
    forward(0)
    load_wo.wait()

    def prepare():
        halo(xn, 0).wait_recv()
        halo(xn, 1).wait_recv()
        for e in range(EXT // TILE):
            flip(e, 1)
            cols = slice(e * TILE, (e + 1) * TILE)
            t = xn[cols, :].astype(F32).T.reshape(HALF // 8, 2, 8, TILE)
            for s in range(2):
                xnT[s, :, cols] = t[:, s].reshape(HALF, TILE).astype(BF)
        for b in range(BLK):
            cols = slice(b * TILE, (b + 1) * TILE)
            for p in range(PAIRS):
                o = dot(
                    kvT[D + p * TILE : D + (p + 1) * TILE, b * TILE : b * TILE + KEYS],
                    pr[b * PAIRS + p], 1, 0,
                )
                o = jnp.concatenate([o[0:HDIM, 0:TILE], o[HDIM:, TILE:]], axis=0)
                o = o.reshape(TILE // 16, 2, 8, TILE)
                for s in range(2):
                    attnT[s, p * HDIM : (p + 1) * HDIM, cols] = (
                        o[:, s].reshape(HDIM, TILE).astype(BF)
                    )

    @pl.when(sec < SEC - 1)
    def _():
        forward_last()
        prepare()

    def g_copy(b):
        return pltpu.make_async_remote_copy(
            gout.at[b], g_v.at[b], g_s.at[b], g_r.at[b],
            device_id=(before, dom), device_id_type=MESH,
        )

    def rim(side, h):
        return pltpu.make_async_remote_copy(
            rim_out.at[side, h], rim_in.at[side, h], rim_ss.at[side, h], rim_rs.at[side, h],
            device_id=(sec, partner if side == 0 else other), device_id_type=MESH,
        )

    def wait_g(b):
        @pl.when(sec == SEC - 1)
        def _():
            load_g[b].wait()

        @pl.when(sec < SEC - 1)
        def _():
            g_copy(b).wait_recv()

    def step(b):
        da = dot(g_v[b], wo[...], 1, 1).astype(BF).astype(F32)
        for p in range(PAIRS):
            db = da[:, p * TILE : (p + 1) * TILE]
            da2[b * PAIRS + p, 0:TILE, :] = (db * m0).astype(BF)
            da2[b * PAIRS + p, TILE:, :] = (db * m1).astype(BF)

        def add(slots, term, off, p):
            cols = slice(off + p * TILE, off + (p + 1) * TILE)
            for n, t in enumerate(slots):
                rows = slice((b + t) * TILE, (b + t + 1) * TILE)
                val = term[n * TILE : (n + 1) * TILE]
                if b == 0 or t == 2:
                    acc[rows, cols] = val
                else:
                    acc[rows, cols] = acc[rows, cols] + val

        edge, rest = {0: ((0,), (1, 2)), 1: ((), (0, 1, 2)), 2: ((2,), (0, 1))}[b]
        at = slice(0, 0) if b == 1 else slice(edge[0] * TILE, (edge[0] + 1) * TILE)
        inner = slice(rest[0] * TILE, (rest[-1] + 1) * TILE)
        side = b // 2
        if b != 1:
            for p in range(PAIRS):
                term = dot(pr[b * PAIRS + p, at, :], da2[b * PAIRS + p], 1, 0)
                add(edge, term, D, p)
                rim_out[side, 1, :, p * TILE : (p + 1) * TILE] = term.astype(BF)
            rim(side, 1).start()
        for p in range(PAIRS):
            vals = kv[b * TILE : b * TILE + KEYS, D + p * TILE : D + (p + 1) * TILE]
            dp = dot(vals, da2[b * PAIRS + p], 1, 1)
            pf = pr[b * PAIRS + p].astype(F32)
            delta = jnp.sum(dp * pf, axis=0, keepdims=True)
            ds = (pf * (dp - delta)).astype(BF)
            dsc[p] = ds
            if b != 1:
                term = dot(ds[at], q2[b * PAIRS + p], 1, 0)
                add(edge, term, 0, p)
                rim_out[side, 0, :, p * TILE : (p + 1) * TILE] = term.astype(BF)
        if b != 1:
            rim(side, 0).start()
        for p in range(PAIRS):
            add(rest, dot(pr[b * PAIRS + p, inner, :], da2[b * PAIRS + p], 1, 0), D, p)
            add(rest, dot(dsc[p, inner, :], q2[b * PAIRS + p], 1, 0), 0, p)
            dq = dot(kvT[p * TILE : (p + 1) * TILE, b * TILE : b * TILE + KEYS], dsc[p], 1, 0)
            dq = jnp.concatenate([dq[0:HDIM, 0:TILE], dq[HDIM:, TILE:]], axis=0)
            dqkv[b * TILE : (b + 1) * TILE, p * TILE : (p + 1) * TILE] = (dq.T * SCALE).astype(BF)

    def close(b):
        dkv = acc[(b + 1) * TILE : (b + 2) * TILE, :]
        if b != 1:
            side = b // 2
            rim(side, 0).wait_recv()
            rim(side, 1).wait_recv()
            dkv = dkv + jnp.concatenate([rim_in[side, 0], rim_in[side, 1]], axis=1).astype(F32)
        dqkv[b * TILE : (b + 1) * TILE, D:] = dkv.astype(BF)

    def finish(b):
        rows = pl.ds(b * TILE, TILE)
        dn = dot(dqkv[rows, :], wq[...], 1, 1)
        xh = xhat[rows, :]
        inv = inv_v[rows, 0:1]
        ln = inv * (
            dn
            - jnp.mean(dn, axis=-1, keepdims=True)
            - xh * jnp.mean(dn * xh, axis=-1, keepdims=True)
        )
        gout[b] = (g_v[b].astype(F32) + ln).astype(BF)

    def store(b):
        return pltpu.make_async_copy(gout.at[b], gout_hbm.at[place(b)], out_sem.at[b])

    def pass_on(b):
        close(b)
        finish(b)
        g_copy(b).start()
        store(b).start()

    def c_copy(j):
        send, recv, _, ss, rs = cores[j]
        return pltpu.make_async_remote_copy(
            send, recv, ss, rs, device_id=(sec, partner), device_id_type=MESH
        )

    def axis_copy(j, stage, o):
        first = CHUNKS[j][2]
        axis = first if stage == 0 else ("z" if first == "y" else "y")
        refs = (firsts if stage == 0 else seconds)[j]
        send, recv, ss, rs = refs[0], refs[1], refs[-2], refs[-1]
        to = y_dev(o) if axis == "y" else z_dev(o)
        return pltpu.make_async_remote_copy(
            send.at[o - 1], recv.at[o - 1], ss.at[o - 1], rs.at[o - 1],
            device_id=(sec, to), device_id_type=MESH,
        )

    def multiply(j, who):
        off, width, _ = CHUNKS[j]
        if off == 3 * D:
            return dot(attnT[who], g_v[...].reshape(ROWS, D), 1, 0)
        if off == 0:
            return dot(xnT[who, :, TILE : TILE + ROWS], dqkv[:, 0:D], 1, 0)
        return dot(xnT[who], accb[:, off - D : off - D + width], 1, 0)

    def open_sum(j):
        cores[j][0][...] = multiply(j, 1 - c).astype(BF)
        c_copy(j).start()
        cores[j][2][...] = multiply(j, c).reshape(NY, NZ, 8, CHUNKS[j][1])

    def first_sum(j):
        width = CHUNKS[j][1]
        c_copy(j).wait_recv()
        held = cores[j][2]
        held[...] = held[...] + cores[j][1][...].astype(F32).reshape(NY, NZ, 8, width)
        send = firsts[j][0]
        if CHUNKS[j][2] == "y":
            for o in range(1, NY):
                send[o - 1] = held[lax.rem(y + o, NY)].reshape(NZ * 8, width).astype(BF)
                axis_copy(j, 0, o).start()
        else:
            for o in range(1, NZ):
                send[o - 1] = held[:, lax.rem(z + o, NZ)].reshape(NY * 8, width).astype(BF)
                axis_copy(j, 0, o).start()

    def fold(piece):
        width = piece.shape[1] // 2
        return jnp.concatenate([piece[:, 0:width], piece[:, width:]], axis=0)

    def second_sum(j):
        width = CHUNKS[j][1]
        held = cores[j][2]
        if CHUNKS[j][2] == "y":
            mine, n1, n2, me = held[y], NY, NZ, z
        else:
            mine, n1, n2, me = held[:, z], NZ, NY, y
        for o in range(1, n1):
            axis_copy(j, 0, o).wait_recv()
            mine = mine + firsts[j][1][o - 1].astype(F32).reshape(n2, 8, width)
        part = firsts[j][2]
        part[...] = mine
        for o in range(1, n2):
            seconds[j][0][o - 1] = fold(part[lax.rem(me + o, n2)]).astype(BF)
            axis_copy(j, 1, o).start()

    def end_sum(j):
        off, width, first = CHUNKS[j]
        me, n2 = (z, NZ) if first == "y" else (y, NY)
        total = fold(firsts[j][2][me])
        for o in range(1, n2):
            axis_copy(j, 1, o).wait_recv()
            total = total + seconds[j][1][o - 1].astype(F32)
        total = jnp.concatenate([total[0:8], total[8:16]], axis=1)
        if off == 3 * D:
            dwo_ref[...] = total
        else:
            dwq_ref[:, off : off + width] = total

    wait_g(0)
    step(0)
    wait_g(1)
    step(1)

    @pl.when(sec > 0)
    def _():
        pass_on(0)

    @pl.when(sec == SEC - 1)
    def _():
        forward_last()

    @pl.when(sec == 0)
    def _():
        wait_g(2)
        open_sum(0)

    @pl.when(sec > 0)
    def _():
        wait_g(2)

    step(2)

    @pl.when(sec > 0)
    def _():
        pass_on(1)
        pass_on(2)

        @pl.when(sec == SEC - 1)
        def _():
            prepare()

        open_sum(0)

    for h in (2, 3, 0, 1):
        cols = slice(h * (D // 2), (h + 1) * (D // 2))
        accb[:, cols] = acc[:, cols].astype(BF)
    for j in range(1, len(CHUNKS)):
        open_sum(j)
    for j in range(len(CHUNKS)):
        first_sum(j)

    @pl.when(sec == 0)
    def _():
        for b in range(BLK):
            close(b)
            finish(b)
            store(b).start()

    for j in range(len(CHUNKS)):
        second_sum(j)
    for j in range(len(CHUNKS)):
        end_sum(j)

    for side in range(2):
        halo(kv, side).wait_send()
        halo(xn, side).wait_send()
        rim(side, 0).wait_send()
        rim(side, 1).wait_send()

    @pl.when(sec > 0)
    def _():
        for b in range(BLK):
            g_copy(b).wait_send()

    for j in range(len(CHUNKS)):
        c_copy(j).wait_send()
        for o in range(1, NY if CHUNKS[j][2] == "y" else NZ):
            axis_copy(j, 0, o).wait_send()
        for o in range(1, NZ if CHUNKS[j][2] == "y" else NY):
            axis_copy(j, 1, o).wait_send()
    for b in range(BLK):
        store(b).wait()


def copy_body(a, b, c, a_out, b_out, c_out):
    a_out[...] = a[...]
    b_out[...] = b[...]
    c_out[...] = c[...]


def local(layer_inputs, top_grad, w_qkv, w_out, neighbours):
    vm = pltpu.VMEM
    sem = pltpu.SemaphoreType.DMA
    anyspec = pl.BlockSpec(memory_space=pl.ANY)
    vspec = pl.BlockSpec(memory_space=pltpu.VMEM)
    outs = (
        jax.ShapeDtypeStruct((BLK, TILE, D), BF),
        jax.ShapeDtypeStruct((D // DOM, 3 * D), F32),
        jax.ShapeDtypeStruct((D // DOM, D), F32),
    )
    cores, firsts, seconds = [], [], []
    for _, width, first in CHUNKS:
        n1, n2 = (NY, NZ) if first == "y" else (NZ, NY)
        cores.append(
            (vm((HALF, width), BF), vm((HALF, width), BF), vm((NY, NZ, 8, width), F32), sem(()), sem(()))
        )
        firsts.append(
            (
                vm((n1 - 1, n2 * 8, width), BF), vm((n1 - 1, n2 * 8, width), BF),
                vm((n2, 8, width), F32), sem((n1 - 1,)), sem((n1 - 1,)),
            )
        )
        seconds.append(
            (
                vm((n2 - 1, 16, width // 2), BF), vm((n2 - 1, 16, width // 2), BF),
                sem((n2 - 1,)), sem((n2 - 1,)),
            )
        )
    results = pl.pallas_call(
        body,
        out_shape=outs,
        in_specs=[pl.BlockSpec(memory_space=pltpu.SMEM)] + [anyspec] * 4,
        out_specs=(anyspec, vspec, vspec),
        scratch_shapes=[
            vm((BLK, TILE, D), BF),
            vm((D, 3 * D), BF),
            vm((D, D), BF),
            vm((BLK, TILE, D), BF),
            vm((ROWS, D), F32),
            vm((ROWS, TILE), F32),
            vm((EXT, D), BF),
            vm((NC, HALF, EXT), BF),
            vm((BLK * PAIRS, 2 * TILE, TILE), BF),
            vm((EXT, 2 * D), BF),
            vm((2 * D, EXT), BF),
            vm((BLK * PAIRS, KEYS, 2 * TILE), BF),
            vm((NC, HALF, ROWS), BF),
            vm((BLK * PAIRS, 2 * TILE, TILE), BF),
            vm((EXT, 2 * D), F32),
            vm((2, 2, TILE, D), BF),
            vm((2, 2, TILE, D), BF),
            vm((EXT, 2 * D), BF),
            vm((PAIRS, KEYS, 2 * TILE), BF),
            vm((ROWS, 3 * D), BF),
            vm((BLK, TILE, D), BF),
            sem((2 * BLK + 2,)), sem((BLK,)),
            sem((4,)), sem((4,)), sem((2, 2)), sem((2, 2)), sem((BLK,)), sem((BLK,)),
            cores, firsts, seconds,
        ],
        compiler_params=pltpu.CompilerParams(
            collective_id=0, has_side_effects=True, vmem_limit_bytes=60 << 20
        ),
        name="layer_backward",
    )(
        neighbours,
        layer_inputs.reshape(BLK, TILE, D),
        top_grad.reshape(BLK, TILE, D),
        w_qkv.reshape(D, 3 * D),
        w_out.reshape(D, D),
    )
    gin, dwq, dwo = pl.pallas_call(
        copy_body,
        out_shape=outs,
        in_specs=[vspec] * 3,
        out_specs=(vspec,) * 3,
        name="results",
    )(*results)
    return (gin.reshape(1, 1, ROWS, D), dwq[None], dwo[None])


def solution(mesh):
    placed = (
        P("section", None, "dom", None),
        P(None, "dom", None),
        P("section", None, None),
        P("section", None, None),
        P("dom", None),
    )
    return jax.shard_map(
        local,
        mesh=mesh,
        in_specs=placed,
        out_specs=(
            P("section", None, "dom", None),
            P("section", "dom", None),
            P("section", "dom", None),
        ),
        check_vma=False,
    )
```

```python
import jax
import jax.numpy as jnp
from jax import lax
from jax.experimental import pallas as pl
from jax.experimental.pallas import tpu as pltpu
from jax.sharding import PartitionSpec as P

SEC = 4
NY, NZ, NC = 4, 8, 2
DOM = NY * NZ * NC
D = 512
HEADS = 8
HDIM = D // HEADS
PAIRS = HEADS // 2
TILE = 128
BLK = 3
KEYS = 3 * TILE
ROWS = BLK * TILE
EXT = ROWS + 2 * TILE
HALF = NY * NZ * 8
SCALE = 1.0 / HDIM**0.5
BF = jnp.bfloat16
F32 = jnp.float32
MESH = pl.DeviceIdType.MESH
CHUNKS = ((1536, 512, "y"), (1024, 512, "z"), (0, 512, "y"), (512, 512, "y"))


def dot(a, b, ca, cb):
    return lax.dot_general(a, b, (((ca,), (cb,)), ((), ())), preferred_element_type=F32)


def body(
    nbr, x_hbm, g_hbm, wq_hbm, wo_hbm, gout_hbm, dwq_ref, dwo_ref,
    x_v, wq, wo, g_v, xhat, inv_v, xn, xnT, q2, kv, kvT, pr, attnT, da2, acc,
    rim_out, rim_in, accb, dsc, dqkv, gout,
    in_sem, out_sem, halo_s, halo_r, rim_ss, rim_rs, g_s, g_r, cores, firsts, seconds,
):
    sec = lax.axis_index("section")
    dom = lax.axis_index("dom")
    y = lax.div(dom, NZ * NC)
    z = lax.rem(lax.div(dom, NC), NZ)
    c = lax.rem(dom, NC)
    other = lax.rem(dom + DOM - 1 + 2 * c, DOM)
    partner = dom + 1 - 2 * c
    before = lax.rem(sec + SEC - 1, SEC)
    after = lax.rem(sec + 1, SEC)

    def place(i):
        return i + (1 - c) * (2 - 2 * i)

    def y_dev(o):
        return lax.rem(y + o, NY) * (NZ * NC) + z * NC + c

    def z_dev(o):
        return y * (NZ * NC) + lax.rem(z + o, NZ) * NC + c

    load_x = [pltpu.make_async_copy(x_hbm.at[place(i)], x_v.at[i], in_sem.at[i]) for i in range(BLK)]
    load_g = [
        pltpu.make_async_copy(g_hbm.at[place(i)], g_v.at[i], in_sem.at[BLK + i]) for i in range(BLK)
    ]
    load_wq = pltpu.make_async_copy(wq_hbm, wq, in_sem.at[2 * BLK])
    load_wo = pltpu.make_async_copy(wo_hbm, wo, in_sem.at[2 * BLK + 1])
    for copy in load_x:
        copy.start()
    load_wq.start()
    load_wo.start()

    @pl.when(sec == SEC - 1)
    def _():
        for copy in load_g:
            copy.start()

    barrier = pltpu.get_barrier_semaphore()
    peers = [(sec, other), (sec, partner), (before, dom), (after, dom)]
    peers += [(sec, y_dev(o)) for o in range(1, NY)]
    peers += [(sec, z_dev(o)) for o in range(1, NZ)]
    for peer in peers:
        pl.semaphore_signal(barrier, inc=1, device_id=peer, device_id_type=MESH)

    lane = lax.broadcasted_iota(jnp.int32, (1, TILE), 1)
    m0 = jnp.where(lane < HDIM, 1.0, 0.0)
    m1 = 1.0 - m0

    for b in range(BLK):
        load_x[b].wait()
        rows = pl.ds(b * TILE, TILE)
        own = pl.ds((b + 1) * TILE, TILE)
        xf = x_v[b].astype(F32)
        cen = xf - jnp.mean(xf, axis=-1, keepdims=True)
        inv = lax.rsqrt(jnp.mean(cen * cen, axis=-1, keepdims=True) + 1e-05)
        xh = cen * inv
        xhat[rows, :] = xh
        inv_v[rows, :] = jnp.broadcast_to(inv, (TILE, TILE))
        xn[own, :] = xh.astype(BF)

    load_wq.wait()
    for h in range(2):
        part = dot(xn[TILE : TILE + ROWS, :], wq[:, (1 + h) * D : (2 + h) * D], 1, 0)
        kv[TILE : TILE + ROWS, h * D : (h + 1) * D] = part.astype(BF)
    pl.semaphore_wait(barrier, len(peers))
    def halo(ref, side):
        sem, to = (0, partner) if side == 0 else (1, other)
        source, target = (TILE, 0) if side == 0 else (ROWS, TILE + ROWS)
        if ref is xn:
            sem = sem + 2
        return pltpu.make_async_remote_copy(
            ref.at[pl.ds(source, TILE)], ref.at[pl.ds(target, TILE)],
            halo_s.at[sem], halo_r.at[sem], device_id=(sec, to), device_id_type=MESH,
        )

    halo(kv, 1).start()
    halo(kv, 0).start()
    halo(xn, 0).start()
    halo(xn, 1).start()

    qs = dot(xn[TILE : TILE + ROWS, :], wq[:, 0:D], 1, 0).astype(BF).astype(F32) * SCALE
    for b in range(BLK):
        for p in range(PAIRS):
            qb = qs[b * TILE : (b + 1) * TILE, p * TILE : (p + 1) * TILE]
            q2[b * PAIRS + p, 0:TILE, :] = (qb * m0).astype(BF)
            q2[b * PAIRS + p, TILE:, :] = (qb * m1).astype(BF)

    def forward(b):
        spot = place(b)
        here = dom * BLK + spot
        low = lax.rem(here + DOM * BLK + 1 - 2 * c, DOM * BLK)
        high = lax.rem(here + DOM * BLK - 1 + 2 * c, DOM * BLK)
        n1 = jnp.full((TILE, 2 * TILE), nbr[spot, 1], jnp.int32)
        n2 = jnp.full((TILE, 2 * TILE), nbr[spot, 2], jnp.int32)
        has_low = (n1 == low) | (n2 == low)
        has_high = (n1 == high) | (n2 == high)
        for p in range(PAIRS):
            keys = kv[b * TILE : b * TILE + KEYS, p * TILE : (p + 1) * TILE]
            s = dot(keys, q2[b * PAIRS + p], 1, 1)
            s = jnp.concatenate(
                [
                    jnp.where(has_low, s[0:TILE], -1e30),
                    s[TILE : 2 * TILE],
                    jnp.where(has_high, s[2 * TILE :], -1e30),
                ],
                axis=0,
            )
            top = jnp.max(s, axis=0, keepdims=True)
            e = jnp.exp(s - top)
            pr[b * PAIRS + p] = (e * (1.0 / jnp.sum(e, axis=0, keepdims=True))).astype(BF)

    def flip(e, h):
        kvT[h * D : (h + 1) * D, e * TILE : (e + 1) * TILE] = kv[
            e * TILE : (e + 1) * TILE, h * D : (h + 1) * D
        ].T

    def forward_last():
        halo(kv, 1).wait_recv()
        flip(4, 0)
        forward(2)

    forward(1)
    for e in range(1, 4):
        flip(e, 0)
    load_wo.wait()

    def prepare():
        halo(xn, 0).wait_recv()
        halo(xn, 1).wait_recv()
        for e in range(EXT // TILE):
            flip(e, 1)
            cols = slice(e * TILE, (e + 1) * TILE)
            t = xn[cols, :].astype(F32).T.reshape(HALF // 8, 2, 8, TILE)
            for s in range(2):
                xnT[s, :, cols] = t[:, s].reshape(HALF, TILE).astype(BF)
        for b in range(BLK):
            cols = slice(b * TILE, (b + 1) * TILE)
            for p in range(PAIRS):
                o = dot(
                    kvT[D + p * TILE : D + (p + 1) * TILE, b * TILE : b * TILE + KEYS],
                    pr[b * PAIRS + p], 1, 0,
                )
                o = jnp.concatenate([o[0:HDIM, 0:TILE], o[HDIM:, TILE:]], axis=0)
                o = o.reshape(TILE // 16, 2, 8, TILE)
                for s in range(2):
                    attnT[s, p * HDIM : (p + 1) * HDIM, cols] = (
                        o[:, s].reshape(HDIM, TILE).astype(BF)
                    )

    def forward_first():
        halo(kv, 0).wait_recv()
        flip(0, 0)
        forward(0)

    @pl.when(sec < SEC - 1)
    def _():
        forward_first()
        forward_last()
        prepare()

    def g_copy(b):
        return pltpu.make_async_remote_copy(
            gout.at[b], g_v.at[b], g_s.at[b], g_r.at[b],
            device_id=(before, dom), device_id_type=MESH,
        )

    def rim(side, h):
        return pltpu.make_async_remote_copy(
            rim_out.at[side, h], rim_in.at[side, h], rim_ss.at[side, h], rim_rs.at[side, h],
            device_id=(sec, partner if side == 0 else other), device_id_type=MESH,
        )

    def wait_g(b):
        @pl.when(sec == SEC - 1)
        def _():
            load_g[b].wait()

        @pl.when(sec < SEC - 1)
        def _():
            g_copy(b).wait_recv()

    def step(b, seen):
        da = dot(g_v[b], wo[...], 1, 1).astype(BF).astype(F32)
        for p in range(PAIRS):
            db = da[:, p * TILE : (p + 1) * TILE]
            da2[b * PAIRS + p, 0:TILE, :] = (db * m0).astype(BF)
            da2[b * PAIRS + p, TILE:, :] = (db * m1).astype(BF)

        def add(slots, term, off, p):
            cols = slice(off + p * TILE, off + (p + 1) * TILE)
            for n, t in enumerate(slots):
                rows = slice((b + t) * TILE, (b + t + 1) * TILE)
                val = term[n * TILE : (n + 1) * TILE]
                if b + t in seen:
                    acc[rows, cols] = acc[rows, cols] + val
                else:
                    acc[rows, cols] = val

        edge, rest = {0: ((0,), (1, 2)), 1: ((), (0, 1, 2)), 2: ((2,), (0, 1))}[b]
        at = slice(0, 0) if b == 1 else slice(edge[0] * TILE, (edge[0] + 1) * TILE)
        inner = slice(rest[0] * TILE, (rest[-1] + 1) * TILE)
        side = b // 2
        if b != 1:
            for p in range(PAIRS):
                term = dot(pr[b * PAIRS + p, at, :], da2[b * PAIRS + p], 1, 0)
                add(edge, term, D, p)
                rim_out[side, 1, :, p * TILE : (p + 1) * TILE] = term.astype(BF)
            rim(side, 1).start()
        for p in range(PAIRS):
            vals = kv[b * TILE : b * TILE + KEYS, D + p * TILE : D + (p + 1) * TILE]
            dp = dot(vals, da2[b * PAIRS + p], 1, 1)
            pf = pr[b * PAIRS + p].astype(F32)
            delta = jnp.sum(dp * pf, axis=0, keepdims=True)
            ds = (pf * (dp - delta)).astype(BF)
            dsc[p] = ds
            if b != 1:
                term = dot(ds[at], q2[b * PAIRS + p], 1, 0)
                add(edge, term, 0, p)
                rim_out[side, 0, :, p * TILE : (p + 1) * TILE] = term.astype(BF)
        if b != 1:
            rim(side, 0).start()
        for p in range(PAIRS):
            add(rest, dot(pr[b * PAIRS + p, inner, :], da2[b * PAIRS + p], 1, 0), D, p)
            add(rest, dot(dsc[p, inner, :], q2[b * PAIRS + p], 1, 0), 0, p)
            dq = dot(kvT[p * TILE : (p + 1) * TILE, b * TILE : b * TILE + KEYS], dsc[p], 1, 0)
            dq = jnp.concatenate([dq[0:HDIM, 0:TILE], dq[HDIM:, TILE:]], axis=0)
            dqkv[b * TILE : (b + 1) * TILE, p * TILE : (p + 1) * TILE] = (dq.T * SCALE).astype(BF)

    def close(b):
        dkv = acc[(b + 1) * TILE : (b + 2) * TILE, :]
        if b != 1:
            side = b // 2
            rim(side, 0).wait_recv()
            rim(side, 1).wait_recv()
            dkv = dkv + jnp.concatenate([rim_in[side, 0], rim_in[side, 1]], axis=1).astype(F32)
        dqkv[b * TILE : (b + 1) * TILE, D:] = dkv.astype(BF)

    def finish(b):
        rows = pl.ds(b * TILE, TILE)
        dn = dot(dqkv[rows, :], wq[...], 1, 1)
        xh = xhat[rows, :]
        inv = inv_v[rows, 0:1]
        ln = inv * (
            dn
            - jnp.mean(dn, axis=-1, keepdims=True)
            - xh * jnp.mean(dn * xh, axis=-1, keepdims=True)
        )
        gout[b] = (g_v[b].astype(F32) + ln).astype(BF)

    def store(b):
        return pltpu.make_async_copy(gout.at[b], gout_hbm.at[place(b)], out_sem.at[b])

    def pass_on(b):
        close(b)
        finish(b)
        g_copy(b).start()
        store(b).start()

    def c_copy(j):
        send, recv, _, ss, rs = cores[j]
        return pltpu.make_async_remote_copy(
            send, recv, ss, rs, device_id=(sec, partner), device_id_type=MESH
        )

    def axis_copy(j, stage, o):
        first = CHUNKS[j][2]
        axis = first if stage == 0 else ("z" if first == "y" else "y")
        refs = (firsts if stage == 0 else seconds)[j]
        send, recv, ss, rs = refs[0], refs[1], refs[-2], refs[-1]
        to = y_dev(o) if axis == "y" else z_dev(o)
        return pltpu.make_async_remote_copy(
            send.at[o - 1], recv.at[o - 1], ss.at[o - 1], rs.at[o - 1],
            device_id=(sec, to), device_id_type=MESH,
        )

    def multiply(j, who):
        off, width, _ = CHUNKS[j]
        if off == 3 * D:
            return dot(attnT[who], g_v[...].reshape(ROWS, D), 1, 0)
        if off == 0:
            return dot(xnT[who, :, TILE : TILE + ROWS], dqkv[:, 0:D], 1, 0)
        return dot(xnT[who], accb[:, off - D : off - D + width], 1, 0)

    def sizes(j):
        return (NY, NZ, y, z) if CHUNKS[j][2] == "y" else (NZ, NY, z, y)

    def by_first(j, val):
        n1, n2, _, _ = sizes(j)
        width = CHUNKS[j][1]
        if CHUNKS[j][2] == "y":
            return val.reshape(n1, n2 * 8, width)
        val = val.reshape(NY, NZ, 8, width)
        return jnp.concatenate([val[i : i + 1] for i in range(NY)], axis=2).reshape(
            n1, n2 * 8, width
        )

    def open_sum(j):
        cores[j][0][...] = by_first(j, multiply(j, 1 - c)).astype(BF)
        c_copy(j).start()

    def own_half(j):
        cores[j][2][...] = by_first(j, multiply(j, c))

    def first_sum(j):
        n1, _, me, _ = sizes(j)
        c_copy(j).wait_recv()
        for o in sorted(range(1, n1), key=lambda o: abs(o - n1 // 2)):
            to = lax.rem(me + o, n1)
            firsts[j][0][o - 1] = (cores[j][2][to] + cores[j][1][to].astype(F32)).astype(BF)
            axis_copy(j, 0, o).start()

    def fold(piece):
        width = piece.shape[1] // 2
        return jnp.concatenate([piece[:, 0:width], piece[:, width:]], axis=0)

    def second_sum(j):
        n1, n2, me1, me = sizes(j)
        mine = cores[j][2][me1] + cores[j][1][me1].astype(F32)
        for o in range(1, n1):
            axis_copy(j, 0, o).wait_recv()
            mine = mine + firsts[j][1][o - 1].astype(F32)
        mine = mine.reshape(n2, 8, CHUNKS[j][1])
        part = firsts[j][2]
        part[...] = mine
        for o in range(1, n2):
            seconds[j][0][o - 1] = fold(part[lax.rem(me + o, n2)]).astype(BF)
            axis_copy(j, 1, o).start()

    def end_sum(j):
        off, width, _ = CHUNKS[j]
        _, n2, _, me = sizes(j)
        total = fold(firsts[j][2][me])
        for o in range(1, n2):
            axis_copy(j, 1, o).wait_recv()
            total = total + seconds[j][1][o - 1].astype(F32)
        total = jnp.concatenate([total[0:8], total[8:16]], axis=1)
        if off == 3 * D:
            dwo_ref[...] = total
        else:
            dwq_ref[:, off : off + width] = total

    @pl.when(sec < SEC - 1)
    def _():
        wait_g(0)
        step(0, ())
        wait_g(1)
        step(1, (1, 2))

    @pl.when(sec == SEC - 1)
    def _():
        wait_g(1)
        step(1, ())
        forward_first()
        wait_g(0)
        step(0, (1, 2))

    @pl.when(sec > 0)
    def _():
        pass_on(0)

    @pl.when(sec == SEC - 1)
    def _():
        forward_last()

    @pl.when(sec == 0)
    def _():
        wait_g(2)
        open_sum(0)
        own_half(0)

    @pl.when(sec > 0)
    def _():
        wait_g(2)

    step(2, (2, 3))

    @pl.when(sec > 0)
    def _():
        pass_on(1)
        pass_on(2)

        @pl.when(sec == SEC - 1)
        def _():
            prepare()

        open_sum(0)
        own_half(0)

    first_sum(0)
    for j in range(1, len(CHUNKS)):
        off, width, _ = CHUNKS[j]
        if off > 0:
            accb[:, off - D : off - D + width] = acc[:, off - D : off - D + width].astype(BF)
        open_sum(j)
    for j in range(1, len(CHUNKS)):
        own_half(j)
    for j in range(1, len(CHUNKS)):
        first_sum(j)

    @pl.when(sec == 0)
    def _():
        for b in range(BLK):
            close(b)
            finish(b)
            store(b).start()

    for j in range(len(CHUNKS)):
        second_sum(j)
    for j in range(len(CHUNKS)):
        end_sum(j)

    for side in range(2):
        halo(kv, side).wait_send()
        halo(xn, side).wait_send()
        rim(side, 0).wait_send()
        rim(side, 1).wait_send()

    @pl.when(sec > 0)
    def _():
        for b in range(BLK):
            g_copy(b).wait_send()

    for j in range(len(CHUNKS)):
        c_copy(j).wait_send()
        for o in range(1, NY if CHUNKS[j][2] == "y" else NZ):
            axis_copy(j, 0, o).wait_send()
        for o in range(1, NZ if CHUNKS[j][2] == "y" else NY):
            axis_copy(j, 1, o).wait_send()
    for b in range(BLK):
        store(b).wait()


def copy_body(a, b, c, a_out, b_out, c_out, a_v, b_v, c_v, in_sem, out_sem):
    parts = [(a.at[i], a_v.at[i], a_out.at[i]) for i in range(BLK)]
    parts += [(b, b_v, b_out), (c, c_v, c_out)]
    loads = [
        pltpu.make_async_copy(src, mid, in_sem.at[i]) for i, (src, mid, _) in enumerate(parts)
    ]
    stores = [
        pltpu.make_async_copy(mid, dst, out_sem.at[i]) for i, (_, mid, dst) in enumerate(parts)
    ]
    for load in loads:
        load.start()
    for load, store in zip(loads, stores):
        load.wait()
        store.start()
    for store in stores:
        store.wait()


def local(layer_inputs, top_grad, w_qkv, w_out, neighbours):
    vm = pltpu.VMEM
    sem = pltpu.SemaphoreType.DMA
    anyspec = pl.BlockSpec(memory_space=pl.ANY)
    vspec = pl.BlockSpec(memory_space=pltpu.VMEM)
    outs = (
        jax.ShapeDtypeStruct((BLK, TILE, D), BF),
        jax.ShapeDtypeStruct((D // DOM, 3 * D), F32),
        jax.ShapeDtypeStruct((D // DOM, D), F32),
    )
    cores, firsts, seconds = [], [], []
    for _, width, first in CHUNKS:
        n1, n2 = (NY, NZ) if first == "y" else (NZ, NY)
        cores.append(
            (vm((n1, n2 * 8, width), BF), vm((n1, n2 * 8, width), BF), vm((n1, n2 * 8, width), F32), sem(()), sem(()))
        )
        firsts.append(
            (
                vm((n1 - 1, n2 * 8, width), BF), vm((n1 - 1, n2 * 8, width), BF),
                vm((n2, 8, width), F32), sem((n1 - 1,)), sem((n1 - 1,)),
            )
        )
        seconds.append(
            (
                vm((n2 - 1, 16, width // 2), BF), vm((n2 - 1, 16, width // 2), BF),
                sem((n2 - 1,)), sem((n2 - 1,)),
            )
        )
    results = pl.pallas_call(
        body,
        out_shape=outs,
        in_specs=[pl.BlockSpec(memory_space=pltpu.SMEM)] + [anyspec] * 4,
        out_specs=(anyspec, vspec, vspec),
        scratch_shapes=[
            vm((BLK, TILE, D), BF),
            vm((D, 3 * D), BF),
            vm((D, D), BF),
            vm((BLK, TILE, D), BF),
            vm((ROWS, D), F32),
            vm((ROWS, TILE), F32),
            vm((EXT, D), BF),
            vm((NC, HALF, EXT), BF),
            vm((BLK * PAIRS, 2 * TILE, TILE), BF),
            vm((EXT, 2 * D), BF),
            vm((2 * D, EXT), BF),
            vm((BLK * PAIRS, KEYS, 2 * TILE), BF),
            vm((NC, HALF, ROWS), BF),
            vm((BLK * PAIRS, 2 * TILE, TILE), BF),
            vm((EXT, 2 * D), F32),
            vm((2, 2, TILE, D), BF),
            vm((2, 2, TILE, D), BF),
            vm((EXT, 2 * D), BF),
            vm((PAIRS, KEYS, 2 * TILE), BF),
            vm((ROWS, 3 * D), BF),
            vm((BLK, TILE, D), BF),
            sem((2 * BLK + 2,)), sem((BLK,)),
            sem((4,)), sem((4,)), sem((2, 2)), sem((2, 2)), sem((BLK,)), sem((BLK,)),
            cores, firsts, seconds,
        ],
        compiler_params=pltpu.CompilerParams(
            collective_id=0, has_side_effects=True, vmem_limit_bytes=60 << 20
        ),
        name="layer_backward",
    )(
        neighbours,
        layer_inputs.reshape(BLK, TILE, D),
        top_grad.reshape(BLK, TILE, D),
        w_qkv.reshape(D, 3 * D),
        w_out.reshape(D, D),
    )
    gin, dwq, dwo = pl.pallas_call(
        copy_body,
        out_shape=outs,
        in_specs=[anyspec] * 3,
        out_specs=(anyspec,) * 3,
        scratch_shapes=[vm(o.shape, o.dtype) for o in outs]
        + [sem((BLK + 2,)), sem((BLK + 2,))],
        name="results",
    )(*results)
    return (gin.reshape(1, 1, ROWS, D), dwq[None], dwo[None])


def solution(mesh):
    placed = (
        P("section", None, "dom", None),
        P(None, "dom", None),
        P("section", None, None),
        P("section", None, None),
        P("dom", None),
    )
    return jax.shard_map(
        local,
        mesh=mesh,
        in_specs=placed,
        out_specs=(
            P("section", None, "dom", None),
            P("section", "dom", None),
            P("section", "dom", None),
        ),
        check_vma=False,
    )
```

```python
import jax
import jax.numpy as jnp
from jax import lax
from jax.experimental import pallas as pl
from jax.experimental.pallas import tpu as pltpu
from jax.sharding import PartitionSpec as P

SEC = 4
NY, NZ, NC = 4, 8, 2
DOM = NY * NZ * NC
D = 512
HEADS = 8
HDIM = D // HEADS
PAIRS = HEADS // 2
TILE = 128
BLK = 3
KEYS = 3 * TILE
ROWS = BLK * TILE
EXT = ROWS + 2 * TILE
HALF = NY * NZ * 8
SCALE = 1.0 / HDIM**0.5
BF = jnp.bfloat16
F32 = jnp.float32
MESH = pl.DeviceIdType.MESH
CHUNKS = ((1536, 512, "y"), (1024, 512, "z"), (0, 512, "y"), (512, 512, "y"))


def dot(a, b, ca, cb):
    return lax.dot_general(a, b, (((ca,), (cb,)), ((), ())), preferred_element_type=F32)


def body(
    nbr, x_hbm, g_hbm, wq_hbm, wo_hbm, gout_hbm, dwq_ref, dwo_ref,
    x_v, wq, wo, g_v, xhat, inv_v, xn, xnT, q2, kv, kvT, pr, attnT, da2, acc,
    rim_out, rim_in, accb, dsc, dqkv, gout,
    in_sem, out_sem, halo_s, halo_r, rim_ss, rim_rs, g_s, g_r, cores, firsts, seconds,
):
    sec = lax.axis_index("section")
    dom = lax.axis_index("dom")
    y = lax.div(dom, NZ * NC)
    z = lax.rem(lax.div(dom, NC), NZ)
    c = lax.rem(dom, NC)
    other = lax.rem(dom + DOM - 1 + 2 * c, DOM)
    partner = dom + 1 - 2 * c
    before = lax.rem(sec + SEC - 1, SEC)
    after = lax.rem(sec + 1, SEC)

    def place(i):
        return i + (1 - c) * (2 - 2 * i)

    def y_dev(o):
        return lax.rem(y + o, NY) * (NZ * NC) + z * NC + c

    def z_dev(o):
        return y * (NZ * NC) + lax.rem(z + o, NZ) * NC + c

    load_x = [pltpu.make_async_copy(x_hbm.at[place(i)], x_v.at[i], in_sem.at[i]) for i in range(BLK)]
    load_g = [
        pltpu.make_async_copy(g_hbm.at[place(i)], g_v.at[i], in_sem.at[BLK + i]) for i in range(BLK)
    ]
    load_wq = pltpu.make_async_copy(wq_hbm, wq, in_sem.at[2 * BLK])
    load_wo = pltpu.make_async_copy(wo_hbm, wo, in_sem.at[2 * BLK + 1])
    for copy in load_x:
        copy.start()
    load_wq.start()
    load_wo.start()

    @pl.when(sec == SEC - 1)
    def _():
        for copy in load_g:
            copy.start()

    barrier = pltpu.get_barrier_semaphore()
    peers = [(sec, other), (sec, partner), (before, dom), (after, dom)]
    peers += [(sec, y_dev(o)) for o in range(1, NY)]
    peers += [(sec, z_dev(o)) for o in range(1, NZ)]
    for peer in peers:
        pl.semaphore_signal(barrier, inc=1, device_id=peer, device_id_type=MESH)

    lane = lax.broadcasted_iota(jnp.int32, (1, TILE), 1)
    m0 = jnp.where(lane < HDIM, 1.0, 0.0)
    m1 = 1.0 - m0

    for b in range(BLK):
        load_x[b].wait()
        rows = pl.ds(b * TILE, TILE)
        own = pl.ds((b + 1) * TILE, TILE)
        xf = x_v[b].astype(F32)
        cen = xf - jnp.mean(xf, axis=-1, keepdims=True)
        inv = lax.rsqrt(jnp.mean(cen * cen, axis=-1, keepdims=True) + 1e-05)
        xh = cen * inv
        xhat[rows, :] = xh
        inv_v[rows, :] = jnp.broadcast_to(inv, (TILE, TILE))
        xn[own, :] = xh.astype(BF)

    load_wq.wait()
    for h in range(2):
        part = dot(xn[TILE : TILE + ROWS, :], wq[:, (1 + h) * D : (2 + h) * D], 1, 0)
        kv[TILE : TILE + ROWS, h * D : (h + 1) * D] = part.astype(BF)
    pl.semaphore_wait(barrier, len(peers))
    def halo(ref, side):
        sem, to = (0, partner) if side == 0 else (1, other)
        source, target = (TILE, 0) if side == 0 else (ROWS, TILE + ROWS)
        if ref is xn:
            sem = sem + 2
        return pltpu.make_async_remote_copy(
            ref.at[pl.ds(source, TILE)], ref.at[pl.ds(target, TILE)],
            halo_s.at[sem], halo_r.at[sem], device_id=(sec, to), device_id_type=MESH,
        )

    halo(kv, 1).start()
    halo(kv, 0).start()
    halo(xn, 0).start()
    halo(xn, 1).start()

    qs = dot(xn[TILE : TILE + ROWS, :], wq[:, 0:D], 1, 0).astype(BF).astype(F32) * SCALE
    for b in range(BLK):
        for p in range(PAIRS):
            qb = qs[b * TILE : (b + 1) * TILE, p * TILE : (p + 1) * TILE]
            q2[b * PAIRS + p, 0:TILE, :] = (qb * m0).astype(BF)
            q2[b * PAIRS + p, TILE:, :] = (qb * m1).astype(BF)

    def forward(b):
        spot = place(b)
        here = dom * BLK + spot
        low = lax.rem(here + DOM * BLK + 1 - 2 * c, DOM * BLK)
        high = lax.rem(here + DOM * BLK - 1 + 2 * c, DOM * BLK)
        n1 = jnp.full((TILE, 2 * TILE), nbr[spot, 1], jnp.int32)
        n2 = jnp.full((TILE, 2 * TILE), nbr[spot, 2], jnp.int32)
        has_low = (n1 == low) | (n2 == low)
        has_high = (n1 == high) | (n2 == high)
        for p in range(PAIRS):
            keys = kv[b * TILE : b * TILE + KEYS, p * TILE : (p + 1) * TILE]
            s = dot(keys, q2[b * PAIRS + p], 1, 1)
            s = jnp.concatenate(
                [
                    jnp.where(has_low, s[0:TILE], -1e30),
                    s[TILE : 2 * TILE],
                    jnp.where(has_high, s[2 * TILE :], -1e30),
                ],
                axis=0,
            )
            top = jnp.max(s, axis=0, keepdims=True)
            e = jnp.exp(s - top)
            pr[b * PAIRS + p] = (e * (1.0 / jnp.sum(e, axis=0, keepdims=True))).astype(BF)

    def flip(e, h):
        kvT[h * D : (h + 1) * D, e * TILE : (e + 1) * TILE] = kv[
            e * TILE : (e + 1) * TILE, h * D : (h + 1) * D
        ].T

    def forward_last():
        halo(kv, 1).wait_recv()
        flip(4, 0)
        forward(2)

    forward(1)
    for e in range(1, 4):
        flip(e, 0)
    load_wo.wait()

    def prepare():
        for e in range(EXT // TILE):
            flip(e, 1)
            cols = slice(e * TILE, (e + 1) * TILE)
            t = xn[cols, :].astype(F32).T.reshape(HALF // 8, 2, 8, TILE)
            for s in range(2):
                xnT[s, :, cols] = t[:, s].reshape(HALF, TILE).astype(BF)
        for b in range(BLK):
            cols = slice(b * TILE, (b + 1) * TILE)
            for p in range(PAIRS):
                o = dot(
                    kvT[D + p * TILE : D + (p + 1) * TILE, b * TILE : b * TILE + KEYS],
                    pr[b * PAIRS + p], 1, 0,
                )
                o = jnp.concatenate([o[0:HDIM, 0:TILE], o[HDIM:, TILE:]], axis=0)
                o = o.reshape(TILE // 16, 2, 8, TILE)
                for s in range(2):
                    attnT[s, p * HDIM : (p + 1) * HDIM, cols] = (
                        o[:, s].reshape(HDIM, TILE).astype(BF)
                    )

    def forward_first():
        halo(kv, 0).wait_recv()
        flip(0, 0)
        forward(0)

    @pl.when(sec < SEC - 1)
    def _():
        forward_first()
        forward_last()
        halo(xn, 0).wait_recv()
        halo(xn, 1).wait_recv()
        prepare()

    def g_copy(b):
        return pltpu.make_async_remote_copy(
            gout.at[b], g_v.at[b], g_s.at[b], g_r.at[b],
            device_id=(before, dom), device_id_type=MESH,
        )

    def rim(side, h):
        return pltpu.make_async_remote_copy(
            rim_out.at[side, h], rim_in.at[side, h], rim_ss.at[side, h], rim_rs.at[side, h],
            device_id=(sec, partner if side == 0 else other), device_id_type=MESH,
        )

    def wait_g(b):
        @pl.when(sec == SEC - 1)
        def _():
            load_g[b].wait()

        @pl.when(sec < SEC - 1)
        def _():
            g_copy(b).wait_recv()

    def project(dn, xh):
        return (
            dn
            - jnp.mean(dn, axis=-1, keepdims=True)
            - xh * jnp.mean(dn * xh, axis=-1, keepdims=True)
        )

    def step(b, seen):
        da = dot(g_v[b], wo[...], 1, 1).astype(BF).astype(F32)
        for p in range(PAIRS):
            db = da[:, p * TILE : (p + 1) * TILE]
            da2[b * PAIRS + p, 0:TILE, :] = (db * m0).astype(BF)
            da2[b * PAIRS + p, TILE:, :] = (db * m1).astype(BF)

        def add(slots, term, off, p):
            cols = slice(off + p * TILE, off + (p + 1) * TILE)
            for n, t in enumerate(slots):
                rows = slice((b + t) * TILE, (b + t + 1) * TILE)
                val = term[n * TILE : (n + 1) * TILE]
                if b + t in seen:
                    acc[rows, cols] = acc[rows, cols] + val
                else:
                    acc[rows, cols] = val

        edge, rest = {0: ((0,), (1, 2)), 1: ((), (0, 1, 2)), 2: ((2,), (0, 1))}[b]
        at = slice(0, 0) if b == 1 else slice(edge[0] * TILE, (edge[0] + 1) * TILE)
        inner = slice(rest[0] * TILE, (rest[-1] + 1) * TILE)
        if b != 1:
            for p in range(PAIRS):
                term = dot(pr[b * PAIRS + p, at, :], da2[b * PAIRS + p], 1, 0)
                add(edge, term, D, p)
                if b == 0:
                    rim_out[0, 1, :, p * TILE : (p + 1) * TILE] = term.astype(BF)
            if b == 0:
                rim(0, 1).start()
        for p in range(PAIRS):
            vals = kv[b * TILE : b * TILE + KEYS, D + p * TILE : D + (p + 1) * TILE]
            dp = dot(vals, da2[b * PAIRS + p], 1, 1)
            pf = pr[b * PAIRS + p].astype(F32)
            delta = jnp.sum(dp * pf, axis=0, keepdims=True)
            ds = (pf * (dp - delta)).astype(BF)
            dsc[p] = ds
            if b != 1:
                term = dot(ds[at], q2[b * PAIRS + p], 1, 0)
                add(edge, term, 0, p)
                if b == 0:
                    rim_out[0, 0, :, p * TILE : (p + 1) * TILE] = term.astype(BF)
        if b == 0:
            rim(0, 0).start()
        if b == 2:
            far = acc[EXT - TILE :, :].astype(BF)
            rim_out[1, 0] = project(
                dot(far, wq[:, D:], 1, 1), xn[EXT - TILE :, :].astype(F32)
            ).astype(BF)
            rim(1, 0).start()
        for p in range(PAIRS):
            add(rest, dot(pr[b * PAIRS + p, inner, :], da2[b * PAIRS + p], 1, 0), D, p)
            add(rest, dot(dsc[p, inner, :], q2[b * PAIRS + p], 1, 0), 0, p)
            dq = dot(kvT[p * TILE : (p + 1) * TILE, b * TILE : b * TILE + KEYS], dsc[p], 1, 0)
            dq = jnp.concatenate([dq[0:HDIM, 0:TILE], dq[HDIM:, TILE:]], axis=0)
            dqkv[b * TILE : (b + 1) * TILE, p * TILE : (p + 1) * TILE] = (dq.T * SCALE).astype(BF)

    def close(b):
        dkv = acc[(b + 1) * TILE : (b + 2) * TILE, :]
        if b == 0:
            rim(0, 0).wait_recv()
            rim(0, 1).wait_recv()
            dkv = dkv + jnp.concatenate([rim_in[0, 0], rim_in[0, 1]], axis=1).astype(F32)
        dqkv[b * TILE : (b + 1) * TILE, D:] = dkv.astype(BF)

    def finish(b):
        rows = pl.ds(b * TILE, TILE)
        dn = dot(dqkv[rows, :], wq[...], 1, 1)
        part = project(dn, xhat[rows, :])
        if b == 2:
            rim(1, 0).wait_recv()
            part = part + rim_in[1, 0].astype(F32)
        ln = inv_v[rows, 0:1] * part
        gout[b] = (g_v[b].astype(F32) + ln).astype(BF)

    def store(b):
        return pltpu.make_async_copy(gout.at[b], gout_hbm.at[place(b)], out_sem.at[b])

    def pass_on(b):
        close(b)
        finish(b)
        g_copy(b).start()
        store(b).start()

    def c_copy(j):
        send, recv, _, ss, rs = cores[j]
        return pltpu.make_async_remote_copy(
            send, recv, ss, rs, device_id=(sec, partner), device_id_type=MESH
        )

    def axis_copy(j, stage, o):
        first = CHUNKS[j][2]
        axis = first if stage == 0 else ("z" if first == "y" else "y")
        refs = (firsts if stage == 0 else seconds)[j]
        send, recv, ss, rs = refs[0], refs[1], refs[-2], refs[-1]
        to = y_dev(o) if axis == "y" else z_dev(o)
        return pltpu.make_async_remote_copy(
            send.at[o - 1], recv.at[o - 1], ss.at[o - 1], rs.at[o - 1],
            device_id=(sec, to), device_id_type=MESH,
        )

    def multiply(j, who):
        off, width, _ = CHUNKS[j]
        if off == 3 * D:
            return dot(attnT[who], g_v[...].reshape(ROWS, D), 1, 0)
        if off == 0:
            return dot(xnT[who, :, TILE : TILE + ROWS], dqkv[:, 0:D], 1, 0)
        return dot(xnT[who], accb[:, off - D : off - D + width], 1, 0)

    def sizes(j):
        return (NY, NZ, y, z) if CHUNKS[j][2] == "y" else (NZ, NY, z, y)

    def by_first(j, val):
        n1, n2, _, _ = sizes(j)
        width = CHUNKS[j][1]
        if CHUNKS[j][2] == "y":
            return val.reshape(n1, n2 * 8, width)
        val = val.reshape(NY, NZ, 8, width)
        return jnp.concatenate([val[i : i + 1] for i in range(NY)], axis=2).reshape(
            n1, n2 * 8, width
        )

    def open_sum(j):
        cores[j][0][...] = by_first(j, multiply(j, 1 - c)).astype(BF)
        c_copy(j).start()

    def own_half(j):
        cores[j][2][...] = by_first(j, multiply(j, c))

    def first_sum(j):
        n1, _, me, _ = sizes(j)
        c_copy(j).wait_recv()
        for o in sorted(range(1, n1), key=lambda o: abs(o - n1 // 2)):
            to = lax.rem(me + o, n1)
            firsts[j][0][o - 1] = (cores[j][2][to] + cores[j][1][to].astype(F32)).astype(BF)
            axis_copy(j, 0, o).start()

    def fold(piece):
        width = piece.shape[1] // 2
        return jnp.concatenate([piece[:, 0:width], piece[:, width:]], axis=0)

    def second_sum(j):
        n1, n2, me1, me = sizes(j)
        mine = cores[j][2][me1] + cores[j][1][me1].astype(F32)
        for o in range(1, n1):
            axis_copy(j, 0, o).wait_recv()
            mine = mine + firsts[j][1][o - 1].astype(F32)
        mine = mine.reshape(n2, 8, CHUNKS[j][1])
        part = firsts[j][2]
        part[...] = mine
        for o in range(1, n2):
            seconds[j][0][o - 1] = fold(part[lax.rem(me + o, n2)]).astype(BF)
            axis_copy(j, 1, o).start()

    def end_sum(j):
        off, width, _ = CHUNKS[j]
        _, n2, _, me = sizes(j)
        total = fold(firsts[j][2][me])
        for o in range(1, n2):
            axis_copy(j, 1, o).wait_recv()
            total = total + seconds[j][1][o - 1].astype(F32)
        total = jnp.concatenate([total[0:8], total[8:16]], axis=1)
        if off == 3 * D:
            dwo_ref[...] = total
        else:
            dwq_ref[:, off : off + width] = total

    @pl.when(sec < SEC - 1)
    def _():
        wait_g(0)
        step(0, ())
        wait_g(1)
        step(1, (1, 2))

    @pl.when(sec == SEC - 1)
    def _():
        wait_g(1)
        step(1, ())
        forward_first()
        wait_g(0)
        step(0, (1, 2))

    @pl.when(sec > 0)
    def _():
        pass_on(0)

    @pl.when(sec == SEC - 1)
    def _():
        forward_last()
        halo(xn, 0).wait_recv()
        halo(xn, 1).wait_recv()

    @pl.when(sec == 0)
    def _():
        wait_g(2)
        open_sum(0)
        own_half(0)

    @pl.when(sec > 0)
    def _():
        wait_g(2)

    step(2, (2, 3))

    @pl.when(sec > 0)
    def _():
        pass_on(1)
        pass_on(2)

        @pl.when(sec == SEC - 1)
        def _():
            prepare()

        open_sum(0)
        own_half(0)

    first_sum(0)
    for j in range(1, len(CHUNKS)):
        off, width, _ = CHUNKS[j]
        if off > 0:
            accb[:, off - D : off - D + width] = acc[:, off - D : off - D + width].astype(BF)
        open_sum(j)
    for j in range(1, len(CHUNKS)):
        own_half(j)
    for j in range(1, len(CHUNKS)):
        first_sum(j)

    @pl.when(sec == 0)
    def _():
        for b in range(BLK):
            close(b)
            finish(b)
            store(b).start()

    for j in range(len(CHUNKS)):
        second_sum(j)
    for j in range(len(CHUNKS)):
        end_sum(j)

    for side in range(2):
        halo(kv, side).wait_send()
        halo(xn, side).wait_send()
        rim(side, 0).wait_send()
    rim(0, 1).wait_send()

    @pl.when(sec > 0)
    def _():
        for b in range(BLK):
            g_copy(b).wait_send()

    for j in range(len(CHUNKS)):
        c_copy(j).wait_send()
        for o in range(1, NY if CHUNKS[j][2] == "y" else NZ):
            axis_copy(j, 0, o).wait_send()
        for o in range(1, NZ if CHUNKS[j][2] == "y" else NY):
            axis_copy(j, 1, o).wait_send()
    for b in range(BLK):
        store(b).wait()


def copy_body(a, b, c, a_out, b_out, c_out, a_v, b_v, c_v, in_sem, out_sem):
    parts = [(a.at[i], a_v.at[i], a_out.at[i]) for i in range(BLK)]
    parts += [(b, b_v, b_out), (c, c_v, c_out)]
    loads = [
        pltpu.make_async_copy(src, mid, in_sem.at[i]) for i, (src, mid, _) in enumerate(parts)
    ]
    stores = [
        pltpu.make_async_copy(mid, dst, out_sem.at[i]) for i, (_, mid, dst) in enumerate(parts)
    ]
    for load in loads:
        load.start()
    for load, store in zip(loads, stores):
        load.wait()
        store.start()
    for store in stores:
        store.wait()


def local(layer_inputs, top_grad, w_qkv, w_out, neighbours):
    vm = pltpu.VMEM
    sem = pltpu.SemaphoreType.DMA
    anyspec = pl.BlockSpec(memory_space=pl.ANY)
    vspec = pl.BlockSpec(memory_space=pltpu.VMEM)
    outs = (
        jax.ShapeDtypeStruct((BLK, TILE, D), BF),
        jax.ShapeDtypeStruct((D // DOM, 3 * D), F32),
        jax.ShapeDtypeStruct((D // DOM, D), F32),
    )
    cores, firsts, seconds = [], [], []
    for _, width, first in CHUNKS:
        n1, n2 = (NY, NZ) if first == "y" else (NZ, NY)
        cores.append(
            (vm((n1, n2 * 8, width), BF), vm((n1, n2 * 8, width), BF), vm((n1, n2 * 8, width), F32), sem(()), sem(()))
        )
        firsts.append(
            (
                vm((n1 - 1, n2 * 8, width), BF), vm((n1 - 1, n2 * 8, width), BF),
                vm((n2, 8, width), F32), sem((n1 - 1,)), sem((n1 - 1,)),
            )
        )
        seconds.append(
            (
                vm((n2 - 1, 16, width // 2), BF), vm((n2 - 1, 16, width // 2), BF),
                sem((n2 - 1,)), sem((n2 - 1,)),
            )
        )
    results = pl.pallas_call(
        body,
        out_shape=outs,
        in_specs=[pl.BlockSpec(memory_space=pltpu.SMEM)] + [anyspec] * 4,
        out_specs=(anyspec, vspec, vspec),
        scratch_shapes=[
            vm((BLK, TILE, D), BF),
            vm((D, 3 * D), BF),
            vm((D, D), BF),
            vm((BLK, TILE, D), BF),
            vm((ROWS, D), F32),
            vm((ROWS, TILE), F32),
            vm((EXT, D), BF),
            vm((NC, HALF, EXT), BF),
            vm((BLK * PAIRS, 2 * TILE, TILE), BF),
            vm((EXT, 2 * D), BF),
            vm((2 * D, EXT), BF),
            vm((BLK * PAIRS, KEYS, 2 * TILE), BF),
            vm((NC, HALF, ROWS), BF),
            vm((BLK * PAIRS, 2 * TILE, TILE), BF),
            vm((EXT, 2 * D), F32),
            vm((2, 2, TILE, D), BF),
            vm((2, 2, TILE, D), BF),
            vm((EXT, 2 * D), BF),
            vm((PAIRS, KEYS, 2 * TILE), BF),
            vm((ROWS, 3 * D), BF),
            vm((BLK, TILE, D), BF),
            sem((2 * BLK + 2,)), sem((BLK,)),
            sem((4,)), sem((4,)), sem((2, 2)), sem((2, 2)), sem((BLK,)), sem((BLK,)),
            cores, firsts, seconds,
        ],
        compiler_params=pltpu.CompilerParams(
            collective_id=0, has_side_effects=True, vmem_limit_bytes=60 << 20
        ),
        name="layer_backward",
    )(
        neighbours,
        layer_inputs.reshape(BLK, TILE, D),
        top_grad.reshape(BLK, TILE, D),
        w_qkv.reshape(D, 3 * D),
        w_out.reshape(D, D),
    )
    gin, dwq, dwo = pl.pallas_call(
        copy_body,
        out_shape=outs,
        in_specs=[anyspec] * 3,
        out_specs=(anyspec,) * 3,
        scratch_shapes=[vm(o.shape, o.dtype) for o in outs]
        + [sem((BLK + 2,)), sem((BLK + 2,))],
        name="results",
    )(*results)
    return (gin.reshape(1, 1, ROWS, D), dwq[None], dwo[None])


def solution(mesh):
    placed = (
        P("section", None, "dom", None),
        P(None, "dom", None),
        P("section", None, None),
        P("section", None, None),
        P("dom", None),
    )
    return jax.shard_map(
        local,
        mesh=mesh,
        in_specs=placed,
        out_specs=(
            P("section", None, "dom", None),
            P("section", "dom", None),
            P("section", "dom", None),
        ),
        check_vma=False,
    )
```

```python
import jax
import jax.numpy as jnp
from jax import lax
from jax.experimental import pallas as pl
from jax.experimental.pallas import tpu as pltpu
from jax.sharding import PartitionSpec as P

SEC = 4
NY, NZ, NC = 4, 8, 2
DOM = NY * NZ * NC
D = 512
HEADS = 8
HDIM = D // HEADS
PAIRS = HEADS // 2
TILE = 128
BLK = 3
KEYS = 3 * TILE
ROWS = BLK * TILE
EXT = ROWS + 2 * TILE
HALF = NY * NZ * 8
SCALE = 1.0 / HDIM**0.5
BF = jnp.bfloat16
F32 = jnp.float32
MESH = pl.DeviceIdType.MESH
CHUNKS = ((1536, 512, "y"), (1024, 512, "z"), (0, 512, "y"), (512, 512, "y"))


def dot(a, b, ca, cb):
    return lax.dot_general(a, b, (((ca,), (cb,)), ((), ())), preferred_element_type=F32)


def body(
    nbr, x_hbm, g_hbm, wq_hbm, wo_hbm, gout_hbm, dwq_ref, dwo_ref,
    x_v, wq, wo, g_v, xhat, inv_v, xn, xnT, q2, kv, kvT, pr, attnT, da2, acc,
    rim_out, rim_in, accb, dsc, dqkv, gout,
    in_sem, out_sem, halo_s, halo_r, rim_ss, rim_rs, g_s, g_r, cores, firsts, seconds,
):
    sec = lax.axis_index("section")
    dom = lax.axis_index("dom")
    y = lax.div(dom, NZ * NC)
    z = lax.rem(lax.div(dom, NC), NZ)
    c = lax.rem(dom, NC)
    other = lax.rem(dom + DOM - 1 + 2 * c, DOM)
    partner = dom + 1 - 2 * c
    before = lax.rem(sec + SEC - 1, SEC)
    after = lax.rem(sec + 1, SEC)

    def place(i):
        return i + (1 - c) * (2 - 2 * i)

    def y_dev(o):
        return lax.rem(y + o, NY) * (NZ * NC) + z * NC + c

    def z_dev(o):
        return y * (NZ * NC) + lax.rem(z + o, NZ) * NC + c

    load_x = [pltpu.make_async_copy(x_hbm.at[place(i)], x_v.at[i], in_sem.at[i]) for i in range(BLK)]
    load_g = [
        pltpu.make_async_copy(g_hbm.at[place(i)], g_v.at[i], in_sem.at[BLK + i]) for i in range(BLK)
    ]
    load_wq = pltpu.make_async_copy(wq_hbm, wq, in_sem.at[2 * BLK])
    load_wo = pltpu.make_async_copy(wo_hbm, wo, in_sem.at[2 * BLK + 1])
    for copy in load_x:
        copy.start()
    load_wq.start()
    load_wo.start()

    @pl.when(sec == SEC - 1)
    def _():
        for copy in load_g:
            copy.start()

    barrier = pltpu.get_barrier_semaphore()
    peers = [(sec, other), (sec, partner), (before, dom), (after, dom)]
    peers += [(sec, y_dev(o)) for o in range(1, NY)]
    peers += [(sec, z_dev(o)) for o in range(1, NZ)]
    for peer in peers:
        pl.semaphore_signal(barrier, inc=1, device_id=peer, device_id_type=MESH)

    lane = lax.broadcasted_iota(jnp.int32, (1, TILE), 1)
    m0 = jnp.where(lane < HDIM, 1.0, 0.0)
    m1 = 1.0 - m0

    for b in range(BLK):
        load_x[b].wait()
        rows = pl.ds(b * TILE, TILE)
        own = pl.ds((b + 1) * TILE, TILE)
        xf = x_v[b].astype(F32)
        cen = xf - jnp.mean(xf, axis=-1, keepdims=True)
        inv = lax.rsqrt(jnp.mean(cen * cen, axis=-1, keepdims=True) + 1e-05)
        xh = cen * inv
        xhat[rows, :] = xh
        inv_v[rows, :] = jnp.broadcast_to(inv, (TILE, TILE))
        xn[own, :] = xh.astype(BF)

    load_wq.wait()
    for h in range(2):
        part = dot(xn[TILE : TILE + ROWS, :], wq[:, (1 + h) * D : (2 + h) * D], 1, 0)
        kv[TILE : TILE + ROWS, h * D : (h + 1) * D] = part.astype(BF)
    pl.semaphore_wait(barrier, len(peers))
    def halo(ref, side):
        sem, to = (0, partner) if side == 0 else (1, other)
        source, target = (TILE, 0) if side == 0 else (ROWS, TILE + ROWS)
        if ref is xn:
            sem = sem + 2
        return pltpu.make_async_remote_copy(
            ref.at[pl.ds(source, TILE)], ref.at[pl.ds(target, TILE)],
            halo_s.at[sem], halo_r.at[sem], device_id=(sec, to), device_id_type=MESH,
        )

    halo(kv, 1).start()
    halo(kv, 0).start()
    halo(xn, 0).start()
    halo(xn, 1).start()

    qs = dot(xn[TILE : TILE + ROWS, :], wq[:, 0:D], 1, 0).astype(BF).astype(F32) * SCALE
    for b in range(BLK):
        for p in range(PAIRS):
            qb = qs[b * TILE : (b + 1) * TILE, p * TILE : (p + 1) * TILE]
            q2[b * PAIRS + p, 0:TILE, :] = (qb * m0).astype(BF)
            q2[b * PAIRS + p, TILE:, :] = (qb * m1).astype(BF)

    def forward(b):
        spot = place(b)
        here = dom * BLK + spot
        low = lax.rem(here + DOM * BLK + 1 - 2 * c, DOM * BLK)
        high = lax.rem(here + DOM * BLK - 1 + 2 * c, DOM * BLK)
        n1 = jnp.full((TILE, 2 * TILE), nbr[spot, 1], jnp.int32)
        n2 = jnp.full((TILE, 2 * TILE), nbr[spot, 2], jnp.int32)
        has_low = (n1 == low) | (n2 == low)
        has_high = (n1 == high) | (n2 == high)
        for p in range(PAIRS):
            keys = kv[b * TILE : b * TILE + KEYS, p * TILE : (p + 1) * TILE]
            s = dot(keys, q2[b * PAIRS + p], 1, 1)
            s = jnp.concatenate(
                [
                    jnp.where(has_low, s[0:TILE], -1e30),
                    s[TILE : 2 * TILE],
                    jnp.where(has_high, s[2 * TILE :], -1e30),
                ],
                axis=0,
            )
            top = jnp.max(s, axis=0, keepdims=True)
            e = jnp.exp(s - top)
            pr[b * PAIRS + p] = (e * (1.0 / jnp.sum(e, axis=0, keepdims=True))).astype(BF)

    def flip(e, h):
        kvT[h * D : (h + 1) * D, e * TILE : (e + 1) * TILE] = kv[
            e * TILE : (e + 1) * TILE, h * D : (h + 1) * D
        ].T

    def forward_last():
        halo(kv, 1).wait_recv()
        flip(4, 0)
        forward(2)

    forward(1)
    for e in range(1, 4):
        flip(e, 0)
    load_wo.wait()

    def prepare():
        for e in range(EXT // TILE):
            flip(e, 1)
            cols = slice(e * TILE, (e + 1) * TILE)
            t = xn[cols, :].astype(F32).T.reshape(HALF // 8, 2, 8, TILE)
            for s in range(2):
                xnT[s, :, cols] = t[:, s].reshape(HALF, TILE).astype(BF)
        for b in range(BLK):
            cols = slice(b * TILE, (b + 1) * TILE)
            for p in range(PAIRS):
                o = dot(
                    kvT[D + p * TILE : D + (p + 1) * TILE, b * TILE : b * TILE + KEYS],
                    pr[b * PAIRS + p], 1, 0,
                )
                o = jnp.concatenate([o[0:HDIM, 0:TILE], o[HDIM:, TILE:]], axis=0)
                o = o.reshape(TILE // 16, 2, 8, TILE)
                for s in range(2):
                    attnT[s, p * HDIM : (p + 1) * HDIM, cols] = (
                        o[:, s].reshape(HDIM, TILE).astype(BF)
                    )

    def forward_first():
        halo(kv, 0).wait_recv()
        flip(0, 0)
        forward(0)

    @pl.when(sec < SEC - 1)
    def _():
        forward_first()
        forward_last()
        halo(xn, 0).wait_recv()
        halo(xn, 1).wait_recv()
        prepare()

    def g_copy(b):
        return pltpu.make_async_remote_copy(
            gout.at[b], g_v.at[b], g_s.at[b], g_r.at[b],
            device_id=(before, dom), device_id_type=MESH,
        )

    def rim(side, h):
        return pltpu.make_async_remote_copy(
            rim_out.at[side, h], rim_in.at[side, h], rim_ss.at[side, h], rim_rs.at[side, h],
            device_id=(sec, partner if side == 0 else other), device_id_type=MESH,
        )

    def wait_g(b):
        @pl.when(sec == SEC - 1)
        def _():
            load_g[b].wait()

        @pl.when(sec < SEC - 1)
        def _():
            g_copy(b).wait_recv()

    def project(dn, xh):
        return (
            dn
            - jnp.mean(dn, axis=-1, keepdims=True)
            - xh * jnp.mean(dn * xh, axis=-1, keepdims=True)
        )

    def send_far():
        far = acc[EXT - TILE :, :].astype(BF)
        rim_out[1, 0] = project(
            dot(far, wq[:, D:], 1, 1), xn[EXT - TILE :, :].astype(F32)
        ).astype(BF)
        rim(1, 0).start()

    def step(b, seen, last=False):
        da = dot(g_v[b], wo[...], 1, 1).astype(BF).astype(F32)
        for p in range(PAIRS):
            db = da[:, p * TILE : (p + 1) * TILE]
            da2[b * PAIRS + p, 0:TILE, :] = (db * m0).astype(BF)
            da2[b * PAIRS + p, TILE:, :] = (db * m1).astype(BF)

        def add(slots, term, off, p):
            cols = slice(off + p * TILE, off + (p + 1) * TILE)
            for n, t in enumerate(slots):
                rows = slice((b + t) * TILE, (b + t + 1) * TILE)
                val = term[n * TILE : (n + 1) * TILE]
                if b + t in seen:
                    acc[rows, cols] = acc[rows, cols] + val
                else:
                    acc[rows, cols] = val

        edge, rest = {0: ((0,), (1, 2)), 1: ((), (0, 1, 2)), 2: ((2,), (0, 1))}[b]
        at = slice(0, 0) if b == 1 else slice(edge[0] * TILE, (edge[0] + 1) * TILE)
        inner = slice(rest[0] * TILE, (rest[-1] + 1) * TILE)
        if b != 1:
            for p in range(PAIRS):
                term = dot(pr[b * PAIRS + p, at, :], da2[b * PAIRS + p], 1, 0)
                add(edge, term, D, p)
                if b == 0:
                    rim_out[0, 1, :, p * TILE : (p + 1) * TILE] = term.astype(BF)
            if b == 0:
                rim(0, 1).start()
        for p in range(PAIRS):
            vals = kv[b * TILE : b * TILE + KEYS, D + p * TILE : D + (p + 1) * TILE]
            dp = dot(vals, da2[b * PAIRS + p], 1, 1)
            pf = pr[b * PAIRS + p].astype(F32)
            delta = jnp.sum(dp * pf, axis=0, keepdims=True)
            ds = (pf * (dp - delta)).astype(BF)
            dsc[p] = ds
            if b != 1:
                term = dot(ds[at], q2[b * PAIRS + p], 1, 0)
                add(edge, term, 0, p)
                if b == 0:
                    rim_out[0, 0, :, p * TILE : (p + 1) * TILE] = term.astype(BF)
        if b == 0:
            rim(0, 0).start()
        if b == 2 and not last:
            send_far()
        for p in range(PAIRS):
            add(rest, dot(pr[b * PAIRS + p, inner, :], da2[b * PAIRS + p], 1, 0), D, p)
            add(rest, dot(dsc[p, inner, :], q2[b * PAIRS + p], 1, 0), 0, p)
            dq = dot(kvT[p * TILE : (p + 1) * TILE, b * TILE : b * TILE + KEYS], dsc[p], 1, 0)
            dq = jnp.concatenate([dq[0:HDIM, 0:TILE], dq[HDIM:, TILE:]], axis=0)
            dqkv[b * TILE : (b + 1) * TILE, p * TILE : (p + 1) * TILE] = (dq.T * SCALE).astype(BF)

    def close(b):
        dkv = acc[(b + 1) * TILE : (b + 2) * TILE, :]
        if b == 0:
            rim(0, 0).wait_recv()
            rim(0, 1).wait_recv()
            dkv = dkv + jnp.concatenate([rim_in[0, 0], rim_in[0, 1]], axis=1).astype(F32)
        dqkv[b * TILE : (b + 1) * TILE, D:] = dkv.astype(BF)

    def finish(b):
        rows = pl.ds(b * TILE, TILE)
        dn = dot(dqkv[rows, :], wq[...], 1, 1)
        part = project(dn, xhat[rows, :])
        if b == 2:
            rim(1, 0).wait_recv()
            part = part + rim_in[1, 0].astype(F32)
        ln = inv_v[rows, 0:1] * part
        gout[b] = (g_v[b].astype(F32) + ln).astype(BF)

    def store(b):
        return pltpu.make_async_copy(gout.at[b], gout_hbm.at[place(b)], out_sem.at[b])

    def pass_on(b):
        close(b)
        finish(b)
        g_copy(b).start()
        store(b).start()

    def c_copy(j):
        send, recv, _, ss, rs = cores[j]
        return pltpu.make_async_remote_copy(
            send, recv, ss, rs, device_id=(sec, partner), device_id_type=MESH
        )

    def axis_copy(j, stage, o):
        first = CHUNKS[j][2]
        axis = first if stage == 0 else ("z" if first == "y" else "y")
        refs = (firsts if stage == 0 else seconds)[j]
        send, recv, ss, rs = refs[0], refs[1], refs[-2], refs[-1]
        to = y_dev(o) if axis == "y" else z_dev(o)
        return pltpu.make_async_remote_copy(
            send.at[o - 1], recv.at[o - 1], ss.at[o - 1], rs.at[o - 1],
            device_id=(sec, to), device_id_type=MESH,
        )

    def multiply(j, who):
        off, width, _ = CHUNKS[j]
        if off == 3 * D:
            return dot(attnT[who], g_v[...].reshape(ROWS, D), 1, 0)
        if off == 0:
            return dot(xnT[who, :, TILE : TILE + ROWS], dqkv[:, 0:D], 1, 0)
        return dot(xnT[who], accb[:, off - D : off - D + width], 1, 0)

    def sizes(j):
        return (NY, NZ, y, z) if CHUNKS[j][2] == "y" else (NZ, NY, z, y)

    def by_first(j, val):
        n1, n2, _, _ = sizes(j)
        width = CHUNKS[j][1]
        if CHUNKS[j][2] == "y":
            return val.reshape(n1, n2 * 8, width)
        val = val.reshape(NY, NZ, 8, width)
        return jnp.concatenate([val[i : i + 1] for i in range(NY)], axis=2).reshape(
            n1, n2 * 8, width
        )

    def open_sum(j):
        cores[j][0][...] = by_first(j, multiply(j, 1 - c)).astype(BF)
        c_copy(j).start()

    def own_half(j):
        cores[j][2][...] = by_first(j, multiply(j, c))

    def first_sum(j):
        n1, _, me, _ = sizes(j)
        c_copy(j).wait_recv()
        for o in sorted(range(1, n1), key=lambda o: abs(o - n1 // 2)):
            to = lax.rem(me + o, n1)
            firsts[j][0][o - 1] = (cores[j][2][to] + cores[j][1][to].astype(F32)).astype(BF)
            axis_copy(j, 0, o).start()

    def fold(piece):
        width = piece.shape[1] // 2
        return jnp.concatenate([piece[:, 0:width], piece[:, width:]], axis=0)

    def second_sum(j):
        n1, n2, me1, me = sizes(j)
        mine = cores[j][2][me1] + cores[j][1][me1].astype(F32)
        for o in range(1, n1):
            axis_copy(j, 0, o).wait_recv()
            mine = mine + firsts[j][1][o - 1].astype(F32)
        mine = mine.reshape(n2, 8, CHUNKS[j][1])
        part = firsts[j][2]
        part[...] = mine
        for o in range(1, n2):
            seconds[j][0][o - 1] = fold(part[lax.rem(me + o, n2)]).astype(BF)
            axis_copy(j, 1, o).start()

    def end_sum(j):
        off, width, _ = CHUNKS[j]
        _, n2, _, me = sizes(j)
        total = fold(firsts[j][2][me])
        for o in range(1, n2):
            axis_copy(j, 1, o).wait_recv()
            total = total + seconds[j][1][o - 1].astype(F32)
        total = jnp.concatenate([total[0:8], total[8:16]], axis=1)
        if off == 3 * D:
            dwo_ref[...] = total
        else:
            dwq_ref[:, off : off + width] = total

    @pl.when(sec < SEC - 1)
    def _():
        wait_g(0)
        step(0, ())
        wait_g(1)
        step(1, (1, 2))

    @pl.when(sec == SEC - 1)
    def _():
        wait_g(1)
        step(1, ())
        forward_first()
        wait_g(0)
        step(0, (1, 2))

    @pl.when(sec > 0)
    def _():
        pass_on(0)

    @pl.when(sec == SEC - 1)
    def _():
        forward_last()
        halo(xn, 0).wait_recv()
        halo(xn, 1).wait_recv()

    @pl.when(sec == 0)
    def _():
        wait_g(2)
        open_sum(0)
        own_half(0)
        step(2, (2, 3), True)

    @pl.when(sec > 0)
    def _():
        wait_g(2)
        step(2, (2, 3))

    @pl.when(sec > 0)
    def _():
        pass_on(1)
        pass_on(2)

        @pl.when(sec == SEC - 1)
        def _():
            prepare()

        open_sum(0)
        own_half(0)

    first_sum(0)
    for j in range(1, len(CHUNKS)):
        off, width, _ = CHUNKS[j]
        if off > 0:
            accb[:, off - D : off - D + width] = acc[:, off - D : off - D + width].astype(BF)
        open_sum(j)

    @pl.when(sec == 0)
    def _():
        send_far()

    for j in range(1, len(CHUNKS)):
        own_half(j)
    for j in range(1, len(CHUNKS)):
        first_sum(j)

    @pl.when(sec == 0)
    def _():
        for b in range(BLK):
            close(b)
            finish(b)
            store(b).start()

    for j in range(len(CHUNKS)):
        second_sum(j)
    for j in range(len(CHUNKS)):
        end_sum(j)

    for side in range(2):
        halo(kv, side).wait_send()
        halo(xn, side).wait_send()
        rim(side, 0).wait_send()
    rim(0, 1).wait_send()

    @pl.when(sec > 0)
    def _():
        for b in range(BLK):
            g_copy(b).wait_send()

    for j in range(len(CHUNKS)):
        c_copy(j).wait_send()
        for o in range(1, NY if CHUNKS[j][2] == "y" else NZ):
            axis_copy(j, 0, o).wait_send()
        for o in range(1, NZ if CHUNKS[j][2] == "y" else NY):
            axis_copy(j, 1, o).wait_send()
    for b in range(BLK):
        store(b).wait()


def copy_body(a, b, c, a_out, b_out, c_out, a_v, b_v, c_v, in_sem, out_sem):
    parts = [(a.at[i], a_v.at[i], a_out.at[i]) for i in range(BLK)]
    parts += [(b, b_v, b_out), (c, c_v, c_out)]
    loads = [
        pltpu.make_async_copy(src, mid, in_sem.at[i]) for i, (src, mid, _) in enumerate(parts)
    ]
    stores = [
        pltpu.make_async_copy(mid, dst, out_sem.at[i]) for i, (_, mid, dst) in enumerate(parts)
    ]
    for load in loads:
        load.start()
    for load, store in zip(loads, stores):
        load.wait()
        store.start()
    for store in stores:
        store.wait()


def local(layer_inputs, top_grad, w_qkv, w_out, neighbours):
    vm = pltpu.VMEM
    sem = pltpu.SemaphoreType.DMA
    anyspec = pl.BlockSpec(memory_space=pl.ANY)
    vspec = pl.BlockSpec(memory_space=pltpu.VMEM)
    outs = (
        jax.ShapeDtypeStruct((BLK, TILE, D), BF),
        jax.ShapeDtypeStruct((D // DOM, 3 * D), F32),
        jax.ShapeDtypeStruct((D // DOM, D), F32),
    )
    cores, firsts, seconds = [], [], []
    for _, width, first in CHUNKS:
        n1, n2 = (NY, NZ) if first == "y" else (NZ, NY)
        cores.append(
            (vm((n1, n2 * 8, width), BF), vm((n1, n2 * 8, width), BF), vm((n1, n2 * 8, width), F32), sem(()), sem(()))
        )
        firsts.append(
            (
                vm((n1 - 1, n2 * 8, width), BF), vm((n1 - 1, n2 * 8, width), BF),
                vm((n2, 8, width), F32), sem((n1 - 1,)), sem((n1 - 1,)),
            )
        )
        seconds.append(
            (
                vm((n2 - 1, 16, width // 2), BF), vm((n2 - 1, 16, width // 2), BF),
                sem((n2 - 1,)), sem((n2 - 1,)),
            )
        )
    results = pl.pallas_call(
        body,
        out_shape=outs,
        in_specs=[pl.BlockSpec(memory_space=pltpu.SMEM)] + [anyspec] * 4,
        out_specs=(anyspec, vspec, vspec),
        scratch_shapes=[
            vm((BLK, TILE, D), BF),
            vm((D, 3 * D), BF),
            vm((D, D), BF),
            vm((BLK, TILE, D), BF),
            vm((ROWS, D), F32),
            vm((ROWS, TILE), F32),
            vm((EXT, D), BF),
            vm((NC, HALF, EXT), BF),
            vm((BLK * PAIRS, 2 * TILE, TILE), BF),
            vm((EXT, 2 * D), BF),
            vm((2 * D, EXT), BF),
            vm((BLK * PAIRS, KEYS, 2 * TILE), BF),
            vm((NC, HALF, ROWS), BF),
            vm((BLK * PAIRS, 2 * TILE, TILE), BF),
            vm((EXT, 2 * D), F32),
            vm((2, 2, TILE, D), BF),
            vm((2, 2, TILE, D), BF),
            vm((EXT, 2 * D), BF),
            vm((PAIRS, KEYS, 2 * TILE), BF),
            vm((ROWS, 3 * D), BF),
            vm((BLK, TILE, D), BF),
            sem((2 * BLK + 2,)), sem((BLK,)),
            sem((4,)), sem((4,)), sem((2, 2)), sem((2, 2)), sem((BLK,)), sem((BLK,)),
            cores, firsts, seconds,
        ],
        compiler_params=pltpu.CompilerParams(
            collective_id=0, has_side_effects=True, vmem_limit_bytes=60 << 20
        ),
        name="layer_backward",
    )(
        neighbours,
        layer_inputs.reshape(BLK, TILE, D),
        top_grad.reshape(BLK, TILE, D),
        w_qkv.reshape(D, 3 * D),
        w_out.reshape(D, D),
    )
    gin, dwq, dwo = pl.pallas_call(
        copy_body,
        out_shape=outs,
        in_specs=[anyspec] * 3,
        out_specs=(anyspec,) * 3,
        scratch_shapes=[vm(o.shape, o.dtype) for o in outs]
        + [sem((BLK + 2,)), sem((BLK + 2,))],
        name="results",
    )(*results)
    return (gin.reshape(1, 1, ROWS, D), dwq[None], dwo[None])


def solution(mesh):
    placed = (
        P("section", None, "dom", None),
        P(None, "dom", None),
        P("section", None, None),
        P("section", None, None),
        P("dom", None),
    )
    return jax.shard_map(
        local,
        mesh=mesh,
        in_specs=placed,
        out_specs=(
            P("section", None, "dom", None),
            P("section", "dom", None),
            P("section", "dom", None),
        ),
        check_vma=False,
    )
```
